32 devices in a mesh: runs: 2 (over x), tm: 16 (over z, y, core), pix: 1.
Axes of the slice: x: 2, y: 2, z: 4, core: 2. Of those that a mesh axis runs over, the one named last changes fastest.
Arguments:
- intensity: float32 [2048, 4096], P('tm', ('runs', 'pix')), parts along dimension 1, may hold values from 0.01 to 60
- cycle_label: int32 [4096], P(('runs', 'pix')), parts along dimension 0, may hold values from 0 to 127, as said below
- valid_mask: int32 [4096], P(('runs', 'pix')), parts along dimension 0, may hold values from 0 to 1, as said below
Outputs:
- correlation: float32 [128, 4096], P('tm', ('runs', 'pix')), parts along dimension 1
The draws below stay inside these ranges and needn't reach their ends.
There are 2 independent parts, one for each index of `runs`. The reference program is written for one: setup_inputs(seed, part) draws one part's arguments, and reference() takes and returns one part's arrays. A program takes and returns all parts, laid end to end along the dimension named above; each array names one. Nothing has to cross between parts.
Inputs may be any that keep to these rules, and one draw needn't show every extreme that they name: `cycle_label`: every cycle 0 to 127 is the label of exactly 16 pixels. `valid_mask`: every cycle holds at least one pixel marked 1.
All inputs are finite; a program needn't handle non-finite values.
Results may differ from the reference program's by a relative error of at most 0.0001.
Values sent between devices are 32-bit elements; how exact they have to be, the bound alone decides.
A program may use at most 64 MiB of HBM per device.

```python
import math
import jax
import jax.numpy as jnp
from jax import lax

Q = 128
LEVELS = 8
LAGS = 16
FRAMES = 2048
PIXELS = 2048


def pixel_layout(key):
    folded = jax.random.fold_in(key, 7)
    first_key, second_key = jax.random.split(folded)
    order = jax.random.permutation(first_key, PIXELS).astype(jnp.int32)
    draws_bits = jax.random.randint(second_key, (PIXELS,), 0, 16)
    labels = (order % Q).astype(jnp.int32)
    marked = jnp.where(order < Q, 1, jnp.where(draws_bits != 0, 1, 0)).astype(jnp.int32)
    return (labels, marked)


def draw_cycle_label(key, part):
    labels, marked = pixel_layout(key)
    return labels


def draw_valid_mask(key, part):
    labels, marked = pixel_layout(key)
    return marked


def draw_intensity(key, part):
    keys = jax.random.split(key, 4)
    position = jnp.arange(PIXELS, dtype=jnp.float32) / max(PIXELS - 1, 1)
    rough = jnp.exp(jax.random.uniform(keys[0], (PIXELS,), jnp.float32, math.log(0.5), math.log(2.0)))
    base = (1.0 + 2.0 * position) * rough
    flux = jnp.exp(jax.random.uniform(keys[1], (FRAMES,), jnp.float32, math.log(0.3), math.log(3.0)))
    noise = jax.random.normal(keys[3], (FRAMES, PIXELS), jnp.float32)
    rising = jnp.arange(FRAMES, dtype=jnp.float32) / max(FRAMES - 1, 1)
    contrast = 0.3 * (1.0 + 2.0 * rising)
    memory = jax.random.uniform(keys[2], (PIXELS,), jnp.float32, 0.3, 0.98)
    spread = jnp.sqrt(1.0 - memory * memory)

    def advance(carried, fresh):
        updated = memory * carried + spread * fresh
        return (updated, updated)
    unused, speckle = lax.scan(advance, jnp.zeros((PIXELS,), jnp.float32), noise)
    values = flux[:, None] * base[None, :] * (1.0 + contrast[:, None] * jnp.tanh(speckle))
    return values.astype(jnp.float32)


def setup_inputs(seed: int = 0, part: int = 0) -> dict:
    seeds = jax.random.split(jax.random.key(seed), 4)
    part_splits = jax.random.split(jax.random.fold_in(seeds[3], part), 4)
    intensity = draw_intensity(jax.random.fold_in(jax.random.fold_in(seeds[3], part), 71), part)
    cycle_label = draw_cycle_label(jax.random.fold_in(jax.random.fold_in(seeds[3], part), 71), part)
    valid_mask = draw_valid_mask(jax.random.fold_in(jax.random.fold_in(seeds[3], part), 71), part)
    return dict(intensity=intensity, cycle_label=cycle_label, valid_mask=valid_mask)


def coarsen(series):
    paired = series.reshape(series.shape[0] // 2, 2, series.shape[1])
    return (paired[:, 0] + paired[:, 1]) * 0.5


def level_rows(series, extension, total_frames):
    frames_here = series.shape[0]
    padded = jnp.concatenate([series, extension], axis=0)
    row_list = []
    for offset in range(extension.shape[0] + 1):
        product = series * padded[offset:offset + frames_here]
        row_list.append(jnp.sum(product, axis=0) / (total_frames - offset))
    return row_list


def normalize(intensity, cycle_label, valid_mask):
    valid_flag = valid_mask.astype(jnp.float32)
    member = (cycle_label[:, None] == jnp.arange(Q, dtype=jnp.int32)[None, :]).astype(jnp.float32)
    weighted = member * valid_flag[:, None]
    cycle_sum = jnp.dot(intensity, weighted, precision=lax.Precision.HIGHEST)
    cycle_count = jnp.sum(weighted, axis=0)
    cycle_mean = cycle_sum / cycle_count[None, :]
    per_pixel = jnp.dot(cycle_mean, member.T, precision=lax.Precision.HIGHEST)
    return valid_flag[None, :] * intensity / per_pixel


def reference(intensity, cycle_label, valid_mask):
    series = normalize(intensity, cycle_label, valid_mask)
    row_list = []
    for height in range(LEVELS):
        if height > 0:
            series = coarsen(series)
        extension = jnp.zeros((LAGS - 1, series.shape[1]), jnp.float32)
        row_list = row_list + level_rows(series, extension, series.shape[0])
    return jnp.stack(row_list)
```

```python
import functools
import jax
import jax.numpy as jnp
from jax import lax
from jax.experimental import pallas as pl
from jax.experimental.pallas import tpu as pltpu
from jax.sharding import PartitionSpec as P

Q = 128
LEVELS = 8
LAGS = 16


def coarsen(series):
    paired = series.reshape(series.shape[0] // 2, 2, series.shape[1])
    return (paired[:, 0] + paired[:, 1]) * 0.5


def level_rows(series, extension, total_frames):
    frames_here = series.shape[0]
    row_list = []
    for offset in range(extension.shape[0] + 1):
        inside = min(offset, frames_here)
        total = jnp.sum(series[: frames_here - inside] * series[inside:], axis=0)
        if offset > 0:
            tail_rows = series[frames_here - inside :]
            total = total + jnp.sum(tail_rows * extension[offset - inside : offset], axis=0)
        row_list.append(total / (total_frames - offset))
    return row_list


def pixel_rows(gathered):
    series = gathered[:, 0, :]
    row_list = []
    for height in range(LEVELS):
        if height > 0:
            series = coarsen(series)
        extension = jnp.zeros((LAGS - 1, series.shape[1]), jnp.float32)
        row_list = row_list + level_rows(series, extension, series.shape[0])
    return jnp.stack(row_list)


def body(intensity, cycle_label, valid_mask):
    valid_flag = valid_mask.astype(jnp.float32)
    member = (cycle_label[:, None] == jnp.arange(Q, dtype=jnp.int32)[None, :]).astype(jnp.float32)
    weighted = member * valid_flag[:, None]
    partial_sum = jnp.dot(intensity, weighted, precision=lax.Precision.HIGHEST)
    partial_count = jnp.sum(weighted, axis=0)
    cycle_sum, cycle_count = lax.psum((partial_sum, partial_count), "pix")
    cycle_mean = cycle_sum / cycle_count[None, :]
    per_pixel = lax.dot_general(
        cycle_mean, member, (((1,), (1,)), ((), ())), precision=lax.Precision.HIGHEST
    )
    normed = valid_flag[None, :] * intensity / per_pixel
    devices_tm = lax.axis_size("tm")
    tile_width = normed.shape[1] // devices_tm
    pieces = normed.reshape(normed.shape[0], devices_tm, tile_width)
    rows_local = pixel_rows(lax.all_to_all(pieces, "tm", split_axis=1, concat_axis=0, tiled=True))
    return lax.all_to_all(rows_local, "tm", split_axis=0, concat_axis=1, tiled=True)

LOCAL = 2
CHUNKS = 4
LANES = 128
SUB = 8


def split(x):
    high = x.astype(jnp.bfloat16)
    return high, (x - high.astype(jnp.float32)).astype(jnp.bfloat16)


def fold_rows(parts):
    row = lax.broadcasted_iota(jnp.int32, (SUB, LANES), 0)
    for step in (4, 2, 1):
        keep = (row & step) == 0

        def swap(v, step=step, keep=keep):
            if step == 4:
                return pltpu.roll(v, 4, 0)
            return jnp.where(keep, pltpu.roll(v, SUB - step, 0), pltpu.roll(v, step, 0))

        parts = [
            jnp.where(keep, parts[i], parts[i + step]) + swap(jnp.where(keep, parts[i + step], parts[i]))
            for i in range(step)
        ]
    return parts[0]


def add_lags(ref, c, blocks, sums):
    for b in blocks:
        base = ref[c, pl.ds(b * SUB, SUB), :]
        for k in range(LAGS):
            term = base * ref[c, pl.ds(b * SUB + k, SUB), :]
            sums[k] = term if sums[k] is None else sums[k] + term
    return sums


def halve(ref, c, start, count):
    even = ref[c, pl.ds(start, count, stride=2), :]
    odd = ref[c, pl.ds(start + 1, count, stride=2), :]
    return (even + odd) * 0.5


def kernel(n, frames, x_hbm, lab_hbm, val_hbm, out_ref, *scratch):
    it = iter(scratch)
    x, wt, lab_ref, val_ref = (next(it) for _ in range(4))
    series = [next(it) for _ in range(LOCAL + 1)]
    far = [next(it) for _ in range(LEVELS - LOCAL)]
    keepers, partial, inbox0, inbox1, inbox, result = (next(it) for _ in range(6))
    load_sem, halo_send, halo_recv, hop_send, hop_recv = (next(it) for _ in range(5))
    plane_send, plane_recv, a2a_send, a2a_recv, out_send, out_recv = (next(it) for _ in range(6))
    me = lax.axis_index("tm")
    rows_out = LEVELS * LAGS // n
    total = n * frames
    groups = x.shape[1] // 256
    keep = LOCAL * LAGS // rows_out

    loads = [
        pltpu.make_async_copy(
            x_hbm.at[:, pl.ds(g * 256, 256)], x.at[:, pl.ds(g * 256, 256)], load_sem.at[g]
        )
        for g in range(groups)
    ]
    lists = [
        pltpu.make_async_copy(lab_hbm, lab_ref, load_sem.at[groups]),
        pltpu.make_async_copy(val_hbm, val_ref, load_sem.at[groups + 1]),
    ]
    for copy in lists + loads:
        copy.start()

    barrier = pltpu.get_barrier_semaphore()

    @pl.loop(1, n)
    def _(d):
        pl.semaphore_signal(
            barrier, inc=1, device_id={"tm": lax.rem(me + d, n)}, device_id_type=pl.DeviceIdType.MESH
        )

    for copy in lists:
        copy.wait()
    cycle = lax.broadcasted_iota(jnp.int32, (Q, 256), 0)
    for g in range(groups):
        lab = lab_ref[:, pl.ds(g * 256, 256)]
        val = val_ref[:, pl.ds(g * 256, 256)].astype(jnp.float32)
        wt[g] = jnp.where(lab == cycle, val, 0.0).astype(jnp.bfloat16)
    ones = jnp.ones((16, 256), jnp.bfloat16)
    acc = jnp.zeros((2 * frames + 16, Q), jnp.float32)
    for g in range(groups):
        loads[g].wait()
        lhs = jnp.concatenate([*split(x[:, pl.ds(g * 256, 256)]), ones], axis=0)
        acc = acc + lax.dot_general(
            lhs, wt[g], (((1,), (1,)), ((), ())), preferred_element_type=jnp.float32
        )
    cycle_sum = acc[:frames] + acc[frames : 2 * frames]
    inverse = acc[2 * frames : 2 * frames + 1] / cycle_sum
    lhs = jnp.concatenate(split(inverse), axis=0)
    for g in range(groups):
        parts = jnp.dot(lhs, wt[g], preferred_element_type=jnp.float32)
        scale = parts[:frames] + parts[frames:]
        normed = x[:, pl.ds(g * 256, 256)] * scale
        series[0][2 * g, pl.ds(0, frames), :] = normed[:, :LANES]
        series[0][2 * g + 1, pl.ds(0, frames), :] = normed[:, LANES:]

    def coarse(c, carry):
        for l in range(1, LOCAL + 1):
            series[l][c, pl.ds(0, frames >> l), :] = halve(series[l - 1], c, 0, frames >> l)
        return carry

    lax.fori_loop(0, n, coarse, 0)

    pl.semaphore_wait(barrier, n - 1)

    block = n // CHUNKS

    def halo(l, q):
        first = 0 if l == 0 else SUB
        count = 2 * SUB - first
        return pltpu.make_async_remote_copy(
            src_ref=series[l].at[pl.ds(q * block, block), pl.ds(first, count), :],
            dst_ref=series[l].at[pl.ds(q * block, block), pl.ds((frames >> l) + first, count), :],
            send_sem=halo_send.at[l, q],
            recv_sem=halo_recv.at[l, q],
            device_id={"tm": lax.rem(me + n - 1, n)},
            device_id_type=pl.DeviceIdType.MESH,
        )

    @pl.when(me > 0)
    def _():
        for q in range(CHUNKS):
            for l in range(LOCAL):
                halo(l, q).start()

    @pl.when(me == n - 1)
    def _():
        for l in range(LOCAL):
            first = 0 if l == 0 else SUB
            series[l][:, pl.ds((frames >> l) + first, 2 * SUB - first), :] = jnp.zeros(
                (n, 2 * SUB - first, LANES), jnp.float32
            )

    deep = frames >> LOCAL

    def spread(peer, source):
        return pltpu.make_async_remote_copy(
            src_ref=series[LOCAL].at[peer],
            dst_ref=far[0].at[0, pl.ds(pl.multiple_of(source * deep, SUB), deep), :],
            send_sem=a2a_send.at[peer],
            recv_sem=a2a_recv.at[source],
            device_id={"tm": peer},
            device_id_type=pl.DeviceIdType.MESH,
        )

    @pl.loop(1, n)
    def _(d):
        spread(lax.rem(me + d, n), me).start()

    def inside(c, carry):
        for l in range(LOCAL):
            sums = add_lags(series[l], c, range((frames >> l) // SUB - 2), [None] * LAGS)
            for k in range(LAGS):
                keepers[c, l * LAGS + k] = sums[k]
        return carry

    lax.fori_loop(0, n, inside, 0)

    side, level, plane = lax.rem(me, 2), lax.rem(me // 2, 2), me // keep
    planes = n // keep

    def hop(s, q):
        part = pl.ds(q * block, block)
        if s == 0:
            src, dst = partial.at[1 - side, :, part], inbox0.at[:, part]
        else:
            src, dst = partial.at[side, 1 - level, part], inbox1.at[part]
        return pltpu.make_async_remote_copy(
            src_ref=src,
            dst_ref=dst,
            send_sem=hop_send.at[s, q],
            recv_sem=hop_recv.at[s, q],
            device_id={"tm": me + 1 - 2 * side if s == 0 else me + 2 - 4 * level},
            device_id_type=pl.DeviceIdType.MESH,
        )

    def gather(source, q):
        part = pl.ds(q * block, block)
        return pltpu.make_async_remote_copy(
            src_ref=partial.at[side, level, part],
            dst_ref=inbox.at[source, part],
            send_sem=plane_send.at[q],
            recv_sem=plane_recv.at[source, q],
            device_id={"tm": lax.rem(me, keep)},
            device_id_type=pl.DeviceIdType.MESH,
        )

    def edge(c, carry):
        for l in range(LOCAL):
            here = frames >> l
            if l > 0:
                series[l][c, pl.ds(here, SUB), :] = halve(series[l - 1], c, 2 * here, SUB)
            sums = [keepers[c, l * LAGS + k] for k in range(LAGS)]
            sums = add_lags(series[l], c, range(here // SUB - 2, here // SUB), sums)
            for h in range(LAGS // SUB):
                partial[h, l, c] = fold_rows(sums[h * SUB : (h + 1) * SUB])
        return carry

    for q in range(CHUNKS):

        @pl.when(me < n - 1)
        def _():
            for l in range(LOCAL):
                halo(l, q).wait_recv()

        lax.fori_loop(q * block, (q + 1) * block, edge, 0)
        hop(0, q).start()
    for q in range(CHUNKS):
        part = pl.ds(q * block, block)
        hop(0, q).wait_recv()
        partial[side, :, part] = partial[side, :, part] + inbox0[:, part]
        hop(1, q).start()
    for q in range(CHUNKS):
        part = pl.ds(q * block, block)
        hop(1, q).wait_recv()
        partial[side, level, part] = partial[side, level, part] + inbox1[part]

        @pl.when(plane > 0)
        def _():
            gather(plane, q).start()

    far[0][0, pl.ds(pl.multiple_of(me * deep, SUB), deep), :] = series[LOCAL][me]
    for i in range(LEVELS - LOCAL):
        count = total >> (LOCAL + i)
        far[i][0, pl.ds(count, 2 * SUB), :] = jnp.zeros((2 * SUB, LANES), jnp.float32)

    @pl.loop(1, n)
    def _(d):
        spread(me, lax.rem(me + n - d, n)).wait_recv()

    lag = lax.broadcasted_iota(jnp.int32, (SUB, LANES), 0)

    def weight(l, h):
        return 1.0 / ((total >> l) - h * SUB - lag).astype(jnp.float32)

    for i in range(LEVELS - LOCAL):
        l = LOCAL + i
        count = total >> l
        if i > 0:
            far[i][0, pl.ds(0, count), :] = halve(far[i - 1], 0, 0, count)
        sums = add_lags(far[i], 0, range(count // SUB), [None] * LAGS)
        for h in range(LAGS // SUB):
            result[pl.ds(l * LAGS + h * SUB, SUB), :] = fold_rows(
                sums[h * SUB : (h + 1) * SUB]
            ) * weight(l, h)

    def deliver(peer, source):
        return pltpu.make_async_remote_copy(
            src_ref=result.at[pl.ds(pl.multiple_of(peer * rows_out, SUB), rows_out), :],
            dst_ref=out_ref.at[:, pl.ds(pl.multiple_of(source * LANES, LANES), LANES)],
            send_sem=out_send.at[peer],
            recv_sem=out_recv.at[source],
            device_id={"tm": peer},
            device_id_type=pl.DeviceIdType.MESH,
        )

    @pl.loop(1, n)
    def _(d):
        peer = lax.rem(me + d, n)

        @pl.when(peer >= keep)
        def _():
            deliver(peer, me).start()

    @pl.when(plane == 0)
    def _():
        count = total // (level + 1) - side * SUB
        scale = 1.0 / (count - lag).astype(jnp.float32)
        for q in range(CHUNKS):
            for source in range(1, planes):
                gather(source, q).wait_recv()
            for c in range(q * block, (q + 1) * block):
                rows = partial[side, level, c]
                for source in range(1, planes):
                    rows = rows + inbox[source, c]
                out_ref[:, pl.ds(c * LANES, LANES)] = rows * scale

    @pl.when(me >= keep)
    def _():
        out_ref[:, pl.ds(pl.multiple_of(me * LANES, LANES), LANES)] = result[
            pl.ds(pl.multiple_of(me * rows_out, SUB), rows_out), :
        ]

        @pl.loop(1, n)
        def _(d):
            deliver(me, lax.rem(me + n - d, n)).wait_recv()

    @pl.loop(1, n)
    def _(d):
        peer = lax.rem(me + n - d, n)
        spread(peer, me).wait_send()

        @pl.when(peer >= keep)
        def _():
            deliver(peer, me).wait_send()

    for q in range(CHUNKS):
        hop(0, q).wait_send()
        hop(1, q).wait_send()
    @pl.when(plane > 0)
    def _():
        for q in range(CHUNKS):
            gather(plane, q).wait_send()

    @pl.when(me > 0)
    def _():
        for l in range(LOCAL):
            for q in range(CHUNKS):
                halo(l, q).wait_send()


def kernel_body(n, intensity, cycle_label, valid_mask):
    frames, pixels = intensity.shape
    f32 = jnp.float32
    dma = pltpu.SemaphoreType.DMA
    keep = LOCAL * LAGS * n // (LEVELS * LAGS)
    scratch = [
        pltpu.VMEM((frames, pixels), f32),
        pltpu.VMEM((pixels // 256, Q, 256), jnp.bfloat16),
        pltpu.VMEM((1, pixels), jnp.int32),
        pltpu.VMEM((1, pixels), jnp.int32),
    ]
    scratch += [pltpu.VMEM((n, (frames >> l) + 2 * SUB, LANES), f32) for l in range(LOCAL)]
    scratch += [pltpu.VMEM((n, frames >> LOCAL, LANES), f32)]
    scratch += [
        pltpu.VMEM((1, (n * frames >> l) + 2 * SUB, LANES), f32) for l in range(LOCAL, LEVELS)
    ]
    scratch += [
        pltpu.VMEM((n, LOCAL * LAGS, SUB, LANES), f32),
        pltpu.VMEM((2, 2, n, SUB, LANES), f32),
        pltpu.VMEM((2, n, SUB, LANES), f32),
        pltpu.VMEM((n, SUB, LANES), f32),
        pltpu.VMEM((n // keep, n, SUB, LANES), f32),
        pltpu.VMEM((LEVELS * LAGS, LANES), f32),
        dma((pixels // 256 + 2,)),
        dma((LOCAL, CHUNKS)),
        dma((LOCAL, CHUNKS)),
        dma((2, CHUNKS)),
        dma((2, CHUNKS)),
        dma((CHUNKS,)),
        dma((n // keep, CHUNKS)),
    ] + [dma((n,))] * 4
    vmem = pl.BlockSpec(memory_space=pltpu.VMEM)
    return pl.pallas_call(
        functools.partial(kernel, n, frames),
        out_shape=pltpu.VMEM((LEVELS * LAGS // n, pixels), f32),
        in_specs=[pl.BlockSpec(memory_space=pl.ANY)] * 3,
        out_specs=vmem,
        scratch_shapes=scratch,
        compiler_params=pltpu.CompilerParams(collective_id=0, has_side_effects=True),
        name="multitau",
    )(intensity, cycle_label.reshape(1, pixels), valid_mask.reshape(1, pixels))


def route(intensity, cycle_label, valid_mask):
    n = lax.axis_size("tm")
    frames, pixels = intensity.shape
    fits = (
        lax.axis_size("pix") == 1
        and pixels == n * LANES
        and frames % (SUB << LOCAL) == 0
        and frames >> LOCAL >= 2 * SUB
        and LEVELS * LAGS == n * SUB
    )
    if fits:
        return kernel_body(n, intensity, cycle_label, valid_mask)
    return body(intensity, cycle_label, valid_mask)


def solution(mesh):
    placed = (P("tm", ("runs", "pix")), P(("runs", "pix")), P(("runs", "pix")))
    return jax.shard_map(
        route, mesh=mesh, in_specs=placed, out_specs=P("tm", ("runs", "pix")), check_vma=False
    )
```

```python
import functools
import jax
import jax.numpy as jnp
from jax import lax
from jax.experimental import pallas as pl
from jax.experimental.pallas import tpu as pltpu
from jax.sharding import PartitionSpec as P

Q = 128
LEVELS = 8
LAGS = 16


def coarsen(series):
    paired = series.reshape(series.shape[0] // 2, 2, series.shape[1])
    return (paired[:, 0] + paired[:, 1]) * 0.5


def level_rows(series, extension, total_frames):
    frames_here = series.shape[0]
    row_list = []
    for offset in range(extension.shape[0] + 1):
        inside = min(offset, frames_here)
        total = jnp.sum(series[: frames_here - inside] * series[inside:], axis=0)
        if offset > 0:
            tail_rows = series[frames_here - inside :]
            total = total + jnp.sum(tail_rows * extension[offset - inside : offset], axis=0)
        row_list.append(total / (total_frames - offset))
    return row_list


def pixel_rows(gathered):
    series = gathered[:, 0, :]
    row_list = []
    for height in range(LEVELS):
        if height > 0:
            series = coarsen(series)
        extension = jnp.zeros((LAGS - 1, series.shape[1]), jnp.float32)
        row_list = row_list + level_rows(series, extension, series.shape[0])
    return jnp.stack(row_list)


def body(intensity, cycle_label, valid_mask):
    valid_flag = valid_mask.astype(jnp.float32)
    member = (cycle_label[:, None] == jnp.arange(Q, dtype=jnp.int32)[None, :]).astype(jnp.float32)
    weighted = member * valid_flag[:, None]
    partial_sum = jnp.dot(intensity, weighted, precision=lax.Precision.HIGHEST)
    partial_count = jnp.sum(weighted, axis=0)
    cycle_sum, cycle_count = lax.psum((partial_sum, partial_count), "pix")
    cycle_mean = cycle_sum / cycle_count[None, :]
    per_pixel = lax.dot_general(
        cycle_mean, member, (((1,), (1,)), ((), ())), precision=lax.Precision.HIGHEST
    )
    normed = valid_flag[None, :] * intensity / per_pixel
    devices_tm = lax.axis_size("tm")
    tile_width = normed.shape[1] // devices_tm
    pieces = normed.reshape(normed.shape[0], devices_tm, tile_width)
    rows_local = pixel_rows(lax.all_to_all(pieces, "tm", split_axis=1, concat_axis=0, tiled=True))
    return lax.all_to_all(rows_local, "tm", split_axis=0, concat_axis=1, tiled=True)

LOCAL = 2
CHUNKS = 4
LANES = 128
SUB = 8


def split(x):
    high = x.astype(jnp.bfloat16)
    return high, (x - high.astype(jnp.float32)).astype(jnp.bfloat16)


def fold_rows(parts):
    row = lax.broadcasted_iota(jnp.int32, (SUB, LANES), 0)
    for step in (4, 2, 1):
        keep = (row & step) == 0

        def swap(v, step=step, keep=keep):
            if step == 4:
                return pltpu.roll(v, 4, 0)
            return jnp.where(keep, pltpu.roll(v, SUB - step, 0), pltpu.roll(v, step, 0))

        parts = [
            jnp.where(keep, parts[i], parts[i + step]) + swap(jnp.where(keep, parts[i + step], parts[i]))
            for i in range(step)
        ]
    return parts[0]


def add_lags(ref, c, blocks, sums):
    for b in blocks:
        base = ref[c, pl.ds(b * SUB, SUB), :]
        for k in range(LAGS):
            term = base * ref[c, pl.ds(b * SUB + k, SUB), :]
            sums[k] = term if sums[k] is None else sums[k] + term
    return sums


def halve(ref, c, start, count):
    even = ref[c, pl.ds(start, count, stride=2), :]
    odd = ref[c, pl.ds(start + 1, count, stride=2), :]
    return (even + odd) * 0.5


def kernel(n, frames, x_hbm, lab_hbm, val_hbm, out_ref, *scratch):
    it = iter(scratch)
    x, wt, lab_ref, val_ref = (next(it) for _ in range(4))
    series = [next(it) for _ in range(LOCAL + 1)]
    far = [next(it) for _ in range(LEVELS - LOCAL)]
    keepers, partial, inbox0, inbox1, inbox, result = (next(it) for _ in range(6))
    load_sem, halo_recv, hop_recv, plane_recv, sent, got = (next(it) for _ in range(6))
    me = lax.axis_index("tm")
    rows_out = LEVELS * LAGS // n
    total = n * frames
    groups = x.shape[1] // 256
    keep = LOCAL * LAGS // rows_out

    loads = [
        pltpu.make_async_copy(
            x_hbm.at[:, pl.ds(g * 256, 256)], x.at[:, pl.ds(g * 256, 256)], load_sem.at[g]
        )
        for g in range(groups)
    ]
    lists = [
        pltpu.make_async_copy(lab_hbm, lab_ref, load_sem.at[groups]),
        pltpu.make_async_copy(val_hbm, val_ref, load_sem.at[groups + 1]),
    ]
    for copy in lists + loads:
        copy.start()

    barrier = pltpu.get_barrier_semaphore()

    @pl.loop(1, n)
    def _(d):
        pl.semaphore_signal(
            barrier, inc=1, device_id={"tm": lax.rem(me + d, n)}, device_id_type=pl.DeviceIdType.MESH
        )

    for copy in lists:
        copy.wait()
    cycle = lax.broadcasted_iota(jnp.int32, (Q, 256), 0)
    members = jnp.zeros((Q, 256), jnp.float32)
    for g in range(groups):
        lab = lab_ref[:, pl.ds(g * 256, 256)]
        val = val_ref[:, pl.ds(g * 256, 256)].astype(jnp.float32)
        member = jnp.where(lab == cycle, val, 0.0)
        members = members + member
        wt[g] = jnp.concatenate([member.astype(jnp.bfloat16)] * 2, axis=0)
    acc = jnp.zeros((Q, 2 * frames), jnp.float32)
    for g in range(groups):
        loads[g].wait()
        rhs = jnp.concatenate(split(x[:, pl.ds(g * 256, 256)]), axis=0)
        acc = acc + lax.dot_general(
            wt[g, pl.ds(0, Q)], rhs, (((1,), (1,)), ((), ())), preferred_element_type=jnp.float32
        )
    count = jnp.sum(members, axis=1, keepdims=True)
    inverse = (count / (acc[:, :frames] + acc[:, frames:])).T
    lhs = jnp.concatenate(split(inverse), axis=1)
    for g in range(groups):
        scale = jnp.dot(lhs, wt[g], preferred_element_type=jnp.float32)
        normed = x[:, pl.ds(g * 256, 256)] * scale
        series[0][2 * g, pl.ds(0, frames), :] = normed[:, :LANES]
        series[0][2 * g + 1, pl.ds(0, frames), :] = normed[:, LANES:]

    def coarse(c, carry):
        for l in range(1, LOCAL + 1):
            series[l][c, pl.ds(0, frames >> l), :] = halve(series[l - 1], c, 0, frames >> l)
        return carry

    lax.fori_loop(0, n, coarse, 0)

    pl.semaphore_wait(barrier, n - 1)

    block = n // CHUNKS

    def halo(l, q):
        first = 0 if l == 0 else SUB
        count = 2 * SUB - first
        return pltpu.make_async_remote_copy(
            src_ref=series[l].at[pl.ds(q * block, block), pl.ds(first, count), :],
            dst_ref=series[l].at[pl.ds(q * block, block), pl.ds((frames >> l) + first, count), :],
            send_sem=sent.at[0],
            recv_sem=halo_recv.at[q],
            device_id={"tm": lax.rem(me + n - 1, n)},
            device_id_type=pl.DeviceIdType.MESH,
        )

    @pl.when(me > 0)
    def _():
        for q in range(CHUNKS):
            for l in range(LOCAL):
                halo(l, q).start()

    @pl.when(me == n - 1)
    def _():
        for l in range(LOCAL):
            first = 0 if l == 0 else SUB
            series[l][:, pl.ds((frames >> l) + first, 2 * SUB - first), :] = jnp.zeros(
                (n, 2 * SUB - first, LANES), jnp.float32
            )

    deep = frames >> LOCAL

    def drain(sem, ref):
        pltpu.make_async_copy(ref, ref, sem).wait()

    def spread(peer, source):
        return pltpu.make_async_remote_copy(
            src_ref=series[LOCAL].at[peer],
            dst_ref=far[0].at[0, pl.ds(pl.multiple_of(source * deep, SUB), deep), :],
            send_sem=sent.at[3],
            recv_sem=got.at[0],
            device_id={"tm": peer},
            device_id_type=pl.DeviceIdType.MESH,
        )

    @pl.loop(1, n)
    def _(d):
        spread(lax.rem(me + d, n), me).start()

    def inside(c, carry):
        for l in range(LOCAL):
            sums = add_lags(series[l], c, range((frames >> l) // SUB - 2), [None] * LAGS)
            for k in range(LAGS):
                keepers[c, l * LAGS + k] = sums[k]
        return carry

    lax.fori_loop(0, n, inside, 0)

    side, level, plane = lax.rem(me, 2), lax.rem(me // 2, 2), me // keep
    planes = n // keep

    def hop(s, q):
        part = pl.ds(q * block, block)
        if s == 0:
            src, dst = partial.at[1 - side, :, part], inbox0.at[:, part]
        else:
            src, dst = partial.at[side, 1 - level, part], inbox1.at[part]
        return pltpu.make_async_remote_copy(
            src_ref=src,
            dst_ref=dst,
            send_sem=sent.at[1],
            recv_sem=hop_recv.at[s, q],
            device_id={"tm": me + 1 - 2 * side if s == 0 else me + 2 - 4 * level},
            device_id_type=pl.DeviceIdType.MESH,
        )

    def gather(source, q):
        part = pl.ds(q * block, block)
        return pltpu.make_async_remote_copy(
            src_ref=partial.at[side, level, part],
            dst_ref=inbox.at[source, part],
            send_sem=sent.at[2],
            recv_sem=plane_recv.at[q],
            device_id={"tm": lax.rem(me, keep)},
            device_id_type=pl.DeviceIdType.MESH,
        )

    def edge(c, carry):
        for l in range(LOCAL):
            here = frames >> l
            if l > 0:
                series[l][c, pl.ds(here, SUB), :] = halve(series[l - 1], c, 2 * here, SUB)
            sums = [keepers[c, l * LAGS + k] for k in range(LAGS)]
            sums = add_lags(series[l], c, range(here // SUB - 2, here // SUB), sums)
            for h in range(LAGS // SUB):
                partial[h, l, c] = fold_rows(sums[h * SUB : (h + 1) * SUB])
        return carry

    for q in range(CHUNKS):

        @pl.when(me < n - 1)
        def _():
            rows = 2 * SUB + (LOCAL - 1) * SUB
            drain(halo_recv.at[q], series[0].at[pl.ds(q * block, block), pl.ds(0, rows), :])

        lax.fori_loop(q * block, (q + 1) * block, edge, 0)
        hop(0, q).start()
    for q in range(CHUNKS):
        part = pl.ds(q * block, block)
        hop(0, q).wait_recv()
        partial[side, :, part] = partial[side, :, part] + inbox0[:, part]
        hop(1, q).start()
    for q in range(CHUNKS):
        part = pl.ds(q * block, block)
        hop(1, q).wait_recv()
        partial[side, level, part] = partial[side, level, part] + inbox1[part]

        @pl.when(plane > 0)
        def _():
            gather(plane, q).start()

    far[0][0, pl.ds(pl.multiple_of(me * deep, SUB), deep), :] = series[LOCAL][me]
    for i in range(LEVELS - LOCAL):
        count = total >> (LOCAL + i)
        far[i][0, pl.ds(count, 2 * SUB), :] = jnp.zeros((2 * SUB, LANES), jnp.float32)

    drain(got.at[0], far[0].at[0, pl.ds(0, (n - 1) * deep), :])

    lag = lax.broadcasted_iota(jnp.int32, (SUB, LANES), 0)

    def weight(l, h):
        return 1.0 / ((total >> l) - h * SUB - lag).astype(jnp.float32)

    for i in range(LEVELS - LOCAL):
        l = LOCAL + i
        count = total >> l
        if i > 0:
            far[i][0, pl.ds(0, count), :] = halve(far[i - 1], 0, 0, count)
        sums = add_lags(far[i], 0, range(count // SUB), [None] * LAGS)
        for h in range(LAGS // SUB):
            result[pl.ds(l * LAGS + h * SUB, SUB), :] = fold_rows(
                sums[h * SUB : (h + 1) * SUB]
            ) * weight(l, h)

    def deliver(peer, source):
        return pltpu.make_async_remote_copy(
            src_ref=result.at[pl.ds(pl.multiple_of(peer * rows_out, SUB), rows_out), :],
            dst_ref=out_ref.at[:, pl.ds(pl.multiple_of(source * LANES, LANES), LANES)],
            send_sem=sent.at[4],
            recv_sem=got.at[1],
            device_id={"tm": peer},
            device_id_type=pl.DeviceIdType.MESH,
        )

    @pl.loop(1, n)
    def _(d):
        peer = lax.rem(me + d, n)

        @pl.when(peer >= keep)
        def _():
            deliver(peer, me).start()

    @pl.when(plane == 0)
    def _():
        count = total // (level + 1) - side * SUB
        scale = 1.0 / (count - lag).astype(jnp.float32)
        for q in range(CHUNKS):
            drain(plane_recv.at[q], inbox.at[pl.ds(1, planes - 1), pl.ds(q * block, block)])
            for c in range(q * block, (q + 1) * block):
                rows = partial[side, level, c]
                for source in range(1, planes):
                    rows = rows + inbox[source, c]
                out_ref[:, pl.ds(c * LANES, LANES)] = rows * scale

    @pl.when(me >= keep)
    def _():
        out_ref[:, pl.ds(pl.multiple_of(me * LANES, LANES), LANES)] = result[
            pl.ds(pl.multiple_of(me * rows_out, SUB), rows_out), :
        ]

        drain(got.at[1], out_ref.at[:, pl.ds(0, (n - 1) * LANES)])
        drain(sent.at[4], out_ref.at[:, pl.ds(0, (n - keep - 1) * LANES)])

    @pl.when(me < keep)
    def _():
        drain(sent.at[4], out_ref.at[:, pl.ds(0, (n - keep) * LANES)])

    drain(sent.at[3], far[0].at[0, pl.ds(0, (n - 1) * deep), :])
    drain(sent.at[1], keepers.at[:, pl.ds(0, 3)])

    @pl.when(plane > 0)
    def _():
        drain(sent.at[2], inbox.at[0])

    @pl.when(me > 0)
    def _():
        drain(sent.at[0], series[0].at[:, pl.ds(0, 2 * SUB + (LOCAL - 1) * SUB), :])


def kernel_body(n, intensity, cycle_label, valid_mask):
    frames, pixels = intensity.shape
    f32 = jnp.float32
    dma = pltpu.SemaphoreType.DMA
    keep = LOCAL * LAGS * n // (LEVELS * LAGS)
    scratch = [
        pltpu.VMEM((frames, pixels), f32),
        pltpu.VMEM((pixels // 256, 2 * Q, 256), jnp.bfloat16),
        pltpu.VMEM((1, pixels), jnp.int32),
        pltpu.VMEM((1, pixels), jnp.int32),
    ]
    scratch += [pltpu.VMEM((n, (frames >> l) + 2 * SUB, LANES), f32) for l in range(LOCAL)]
    scratch += [pltpu.VMEM((n, frames >> LOCAL, LANES), f32)]
    scratch += [
        pltpu.VMEM((1, (n * frames >> l) + 2 * SUB, LANES), f32) for l in range(LOCAL, LEVELS)
    ]
    scratch += [
        pltpu.VMEM((n, LOCAL * LAGS, SUB, LANES), f32),
        pltpu.VMEM((2, 2, n, SUB, LANES), f32),
        pltpu.VMEM((2, n, SUB, LANES), f32),
        pltpu.VMEM((n, SUB, LANES), f32),
        pltpu.VMEM((n // keep, n, SUB, LANES), f32),
        pltpu.VMEM((LEVELS * LAGS, LANES), f32),
        dma((pixels // 256 + 2,)),
        dma((CHUNKS,)),
        dma((2, CHUNKS)),
        dma((CHUNKS,)),
        dma((5,)),
        dma((2,)),
    ]
    vmem = pl.BlockSpec(memory_space=pltpu.VMEM)
    return pl.pallas_call(
        functools.partial(kernel, n, frames),
        out_shape=pltpu.VMEM((LEVELS * LAGS // n, pixels), f32),
        in_specs=[pl.BlockSpec(memory_space=pl.ANY)] * 3,
        out_specs=vmem,
        scratch_shapes=scratch,
        compiler_params=pltpu.CompilerParams(collective_id=0, has_side_effects=True),
        name="multitau",
    )(intensity, cycle_label.reshape(1, pixels), valid_mask.reshape(1, pixels))


def route(intensity, cycle_label, valid_mask):
    n = lax.axis_size("tm")
    frames, pixels = intensity.shape
    fits = (
        lax.axis_size("pix") == 1
        and pixels == n * LANES
        and frames % (SUB << LOCAL) == 0
        and frames >> LOCAL >= 2 * SUB
        and LEVELS * LAGS == n * SUB
    )
    if fits:
        return kernel_body(n, intensity, cycle_label, valid_mask)
    return body(intensity, cycle_label, valid_mask)


def solution(mesh):
    placed = (P("tm", ("runs", "pix")), P(("runs", "pix")), P(("runs", "pix")))
    return jax.shard_map(
        route, mesh=mesh, in_specs=placed, out_specs=P("tm", ("runs", "pix")), check_vma=False
    )
```

```python
import functools
import jax
import jax.numpy as jnp
from jax import lax
from jax.experimental import pallas as pl
from jax.experimental.pallas import tpu as pltpu
from jax.sharding import PartitionSpec as P

Q = 128
LEVELS = 8
LAGS = 16


def coarsen(series):
    paired = series.reshape(series.shape[0] // 2, 2, series.shape[1])
    return (paired[:, 0] + paired[:, 1]) * 0.5


def level_rows(series, extension, total_frames):
    frames_here = series.shape[0]
    row_list = []
    for offset in range(extension.shape[0] + 1):
        inside = min(offset, frames_here)
        total = jnp.sum(series[: frames_here - inside] * series[inside:], axis=0)
        if offset > 0:
            tail_rows = series[frames_here - inside :]
            total = total + jnp.sum(tail_rows * extension[offset - inside : offset], axis=0)
        row_list.append(total / (total_frames - offset))
    return row_list


def pixel_rows(gathered):
    series = gathered[:, 0, :]
    row_list = []
    for height in range(LEVELS):
        if height > 0:
            series = coarsen(series)
        extension = jnp.zeros((LAGS - 1, series.shape[1]), jnp.float32)
        row_list = row_list + level_rows(series, extension, series.shape[0])
    return jnp.stack(row_list)


def body(intensity, cycle_label, valid_mask):
    valid_flag = valid_mask.astype(jnp.float32)
    member = (cycle_label[:, None] == jnp.arange(Q, dtype=jnp.int32)[None, :]).astype(jnp.float32)
    weighted = member * valid_flag[:, None]
    partial_sum = jnp.dot(intensity, weighted, precision=lax.Precision.HIGHEST)
    partial_count = jnp.sum(weighted, axis=0)
    cycle_sum, cycle_count = lax.psum((partial_sum, partial_count), "pix")
    cycle_mean = cycle_sum / cycle_count[None, :]
    per_pixel = lax.dot_general(
        cycle_mean, member, (((1,), (1,)), ((), ())), precision=lax.Precision.HIGHEST
    )
    normed = valid_flag[None, :] * intensity / per_pixel
    devices_tm = lax.axis_size("tm")
    tile_width = normed.shape[1] // devices_tm
    pieces = normed.reshape(normed.shape[0], devices_tm, tile_width)
    rows_local = pixel_rows(lax.all_to_all(pieces, "tm", split_axis=1, concat_axis=0, tiled=True))
    return lax.all_to_all(rows_local, "tm", split_axis=0, concat_axis=1, tiled=True)

LOCAL = 2
CHUNKS = (4, 4)
LANES = 128
SUB = 8
HALO = 2 * SUB
UNROLL = 4


def split(x):
    high = x.astype(jnp.bfloat16)
    return high, (x - high.astype(jnp.float32)).astype(jnp.bfloat16)


def fold_rows(parts):
    row = lax.broadcasted_iota(jnp.int32, (SUB, LANES), 0)
    for step in (4, 2, 1):
        keep = (row & step) == 0

        def swap(v, step=step, keep=keep):
            if step == 4:
                return pltpu.roll(v, 4, 0)
            return jnp.where(keep, pltpu.roll(v, SUB - step, 0), pltpu.roll(v, step, 0))

        parts = [
            jnp.where(keep, parts[i], parts[i + step]) + swap(jnp.where(keep, parts[i + step], parts[i]))
            for i in range(step)
        ]
    return parts[0]


def add_lags(ref, c, blocks, sums):
    for b in blocks:
        base = ref[c, pl.ds(b * SUB, SUB), :]
        for k in range(LAGS):
            term = base * ref[c, pl.ds(b * SUB + k, SUB), :]
            sums[k] = term if sums[k] is None else sums[k] + term
    return sums


def each(first, last, step):
    width = UNROLL
    while (last - first) % width:
        width //= 2

    def several(i, carry):
        for k in range(width):
            step(first + i * width + k, carry)
        return carry

    lax.fori_loop(0, (last - first) // width, several, 0)


def halve(ref, c, start, count):
    even = ref[c, pl.ds(start, count, stride=2), :]
    odd = ref[c, pl.ds(start + 1, count, stride=2), :]
    return (even + odd) * 0.5


def kernel(n, frames, x_hbm, lab_hbm, val_hbm, out_ref, *scratch):
    it = iter(scratch)
    x, wt, lab_ref, val_ref = (next(it) for _ in range(4))
    series = [next(it) for _ in range(LOCAL + 1)]
    far = [next(it) for _ in range(LEVELS - LOCAL)]
    keepers, partial, inbox0, inbox1, inbox, result = (next(it) for _ in range(6))
    load_sem, halo_recv, core_recv, pair_recv, plane_recv, sent, got = (next(it) for _ in range(7))
    me = lax.axis_index("tm")
    rows_out = LEVELS * LAGS // n
    total = n * frames
    groups = x.shape[1] // 256
    keep = LOCAL * LAGS // rows_out
    chip = LAGS // rows_out
    stack = 2 * chip
    planes = n // stack
    side, parity, plane = lax.rem(me, chip), lax.rem(me // chip, 2), me // stack

    loads = [
        pltpu.make_async_copy(
            x_hbm.at[:, pl.ds(g * 256, 256)], x.at[:, pl.ds(g * 256, 256)], load_sem.at[g]
        )
        for g in range(groups)
    ]
    lists = [
        pltpu.make_async_copy(lab_hbm, lab_ref, load_sem.at[groups]),
        pltpu.make_async_copy(val_hbm, val_ref, load_sem.at[groups + 1]),
    ]
    for copy in lists + loads:
        copy.start()

    barrier = pltpu.get_barrier_semaphore()

    @pl.loop(1, n)
    def _(d):
        pl.semaphore_signal(
            barrier, inc=1, device_id={"tm": lax.rem(me + d, n)}, device_id_type=pl.DeviceIdType.MESH
        )

    def remote(src, dst, send_sem, recv_sem, target):
        return pltpu.make_async_remote_copy(
            src_ref=src,
            dst_ref=dst,
            send_sem=send_sem,
            recv_sem=recv_sem,
            device_id={"tm": target},
            device_id_type=pl.DeviceIdType.MESH,
        )

    def drain(sem, ref):
        pltpu.make_async_copy(ref, ref, sem).wait()

    before = lax.rem(me + n - 1, n)

    for copy in lists:
        copy.wait()
    cycle = lax.broadcasted_iota(jnp.int32, (Q, 256), 0)
    members = jnp.zeros((Q, 256), jnp.float32)
    for g in range(groups):
        lab = lab_ref[:, pl.ds(g * 256, 256)]
        val = val_ref[:, pl.ds(g * 256, 256)].astype(jnp.float32)
        member = jnp.where(lab == cycle, val, 0.0)
        members = members + member
        wt[g] = jnp.concatenate([member.astype(jnp.bfloat16)] * 2, axis=0)

    acc = jnp.zeros((Q, 2 * frames), jnp.float32)
    for g in range(groups):
        loads[g].wait()
        rhs = jnp.concatenate(split(x[:, pl.ds(g * 256, 256)]), axis=0)
        acc = acc + lax.dot_general(
            wt[g, pl.ds(0, Q)], rhs, (((1,), (1,)), ((), ())), preferred_element_type=jnp.float32
        )
    count = jnp.sum(members, axis=1, keepdims=True)
    inverse = (count / (acc[:, :frames] + acc[:, frames:])).T

    def normalise(first, count):
        lhs = jnp.concatenate(split(inverse[first : first + count]), axis=1)
        for g in range(groups):
            scale = jnp.dot(lhs, wt[g], preferred_element_type=jnp.float32)
            normed = x[pl.ds(first, count), pl.ds(g * 256, 256)] * scale
            series[0][2 * g, pl.ds(first, count), :] = normed[:, :LANES]
            series[0][2 * g + 1, pl.ds(first, count), :] = normed[:, LANES:]

    def halo(l):
        first = 0 if l == 0 else SUB
        return remote(
            series[l].at[:, pl.ds(first, 2 * SUB - first), :],
            series[l].at[:, pl.ds((frames >> l) + first, 2 * SUB - first), :],
            sent.at[0],
            halo_recv.at[l],
            before,
        )

    normalise(0, HALO)
    pl.semaphore_wait(barrier, n - 1)

    @pl.when(me > 0)
    def _():
        halo(0).start()

    normalise(HALO, frames - HALO)

    def coarse(c, carry):
        for l in range(1, LOCAL + 1):
            series[l][c, pl.ds(0, frames >> l), :] = halve(series[l - 1], c, 0, frames >> l)
        return carry

    each(0, n, coarse)

    @pl.when(me > 0)
    def _():
        for l in range(1, LOCAL):
            halo(l).start()

    deep = frames >> LOCAL

    def spread():
        @pl.loop(1, n)
        def _(d):
            peer = lax.rem(me + d, n)
            remote(
                series[LOCAL].at[peer],
                far[0].at[0, pl.ds(pl.multiple_of(me * deep, SUB), deep), :],
                sent.at[2],
                got.at[0],
                peer,
            ).start()

    def inside(l):
        def one(c, carry):
            sums = add_lags(series[l], c, range((frames >> l) // SUB - 2), [None] * LAGS)
            for k in range(LAGS):
                keepers[c, l * LAGS + k] = sums[k]
            return carry

        each(0, n, one)

    inside(0)

    @pl.when(me == n - 1)
    def _():
        for l in range(LOCAL):
            first = 0 if l == 0 else SUB
            series[l][:, pl.ds((frames >> l) + first, 2 * SUB - first), :] = jnp.zeros(
                (n, 2 * SUB - first, LANES), jnp.float32
            )

    def parts(l, q):
        block = n // CHUNKS[l]
        return pl.ds(q * block, block)

    def sem(l, q):
        return sum(CHUNKS[:l]) + q

    def to_core(l, q):
        part = parts(l, q)
        return remote(
            partial.at[1 - side, l, part],
            inbox0.at[l, part],
            sent.at[3],
            core_recv.at[sem(l, q)],
            me + 1 - 2 * side,
        )

    def to_pair(l, q):
        part = parts(l, q)
        return remote(
            partial.at[side, l, part],
            inbox1.at[l // 2, part],
            sent.at[4 + l % 2],
            pair_recv.at[sem(l, q)],
            me + chip - 2 * chip * parity,
        )

    def to_plane(l, q):
        part = parts(l, q)
        return remote(
            partial.at[side, l, part],
            inbox.at[plane, part],
            sent.at[6 + l],
            plane_recv.at[q],
            lax.rem(me, stack) + (l // 2) * stack,
        )

    def edges(l, q):
        here = frames >> l
        block = n // CHUNKS[l]

        def edge(c, carry):
            if l > 0:
                series[l][c, pl.ds(here, SUB), :] = halve(series[l - 1], c, 2 * here, SUB)
            sums = [keepers[c, l * LAGS + k] for k in range(LAGS)]
            sums = add_lags(series[l], c, range(here // SUB - 2, here // SUB), sums)
            for h in range(LAGS // SUB):
                partial[h, l, c] = fold_rows(sums[h * SUB : (h + 1) * SUB])
            return carry

        each(q * block, (q + 1) * block, edge)

    def compute(l):
        if l > 0:
            inside(l)

        @pl.when(me < n - 1)
        def _():
            drain(halo_recv.at[l], series[l].at[:, pl.ds(0, 2 * SUB if l == 0 else SUB), :])

        if l == 0:
            spread()

        for q in range(CHUNKS[l]):
            edges(l, q)
            to_core(l, q).start()

    def across(l):
        for q in range(CHUNKS[l]):
            part = parts(l, q)
            to_core(l, q).wait_recv()
            partial[side, l, part] = partial[side, l, part] + inbox0[l, part]

            @pl.when(parity != l % 2)
            def _():
                to_pair(l, q).start()

    def along(l):
        for q in range(CHUNKS[l]):

            @pl.when(parity == l % 2)
            def _():
                part = parts(l, q)
                to_pair(l, q).wait_recv()
                partial[side, l, part] = partial[side, l, part] + inbox1[l // 2, part]

                @pl.when(plane != l // 2)
                def _():
                    to_plane(l, q).start()

    compute(0)
    compute(1)
    across(0)
    across(1)
    along(0)
    along(1)

    far[0][0, pl.ds(pl.multiple_of(me * deep, SUB), deep), :] = series[LOCAL][me]
    for i in range(LEVELS - LOCAL):
        count = total >> (LOCAL + i)
        far[i][0, pl.ds(count, 2 * SUB), :] = jnp.zeros((2 * SUB, LANES), jnp.float32)
    drain(got.at[0], far[0].at[0, pl.ds(0, (n - 1) * deep), :])
    lag = lax.broadcasted_iota(jnp.int32, (SUB, LANES), 0)

    def weight(l, h):
        return 1.0 / ((total >> l) - h * SUB - lag).astype(jnp.float32)

    for i in range(LEVELS - LOCAL):
        l = LOCAL + i
        count = total >> l
        if i > 0:
            far[i][0, pl.ds(0, count), :] = halve(far[i - 1], 0, 0, count)
        sums = add_lags(far[i], 0, range(count // SUB), [None] * LAGS)
        for h in range(LAGS // SUB):
            result[pl.ds(l * LAGS + h * SUB, SUB), :] = fold_rows(
                sums[h * SUB : (h + 1) * SUB]
            ) * weight(l, h)

    @pl.loop(1, n)
    def _(d):
        peer = lax.rem(me + d, n)

        @pl.when(peer >= keep)
        def _():
            remote(
                result.at[pl.ds(pl.multiple_of(peer * rows_out, SUB), rows_out), :],
                out_ref.at[:, pl.ds(pl.multiple_of(me * LANES, LANES), LANES)],
                sent.at[9],
                got.at[1],
                peer,
            ).start()

    for l in range(LOCAL):

        @pl.when((plane == l // 2) & (parity == l % 2))
        def _():
            scale = 1.0 / ((total >> l) - side * SUB - lag).astype(jnp.float32)
            for q in range(CHUNKS[l]):
                block = n // CHUNKS[l]
                drain(plane_recv.at[q], inbox.at[pl.ds(0, planes - 1), pl.ds(q * block, block)])
                for c in range(q * block, (q + 1) * block):
                    rows = partial[side, l, c]
                    for source in range(planes):
                        if source != l // 2:
                            rows = rows + inbox[source, c]
                    out_ref[:, pl.ds(c * LANES, LANES)] = rows * scale

        @pl.when((plane != l // 2) & (parity == l % 2))
        def _():
            drain(sent.at[6 + l], inbox.at[0])

    @pl.when(me >= keep)
    def _():
        out_ref[:, pl.ds(pl.multiple_of(me * LANES, LANES), LANES)] = result[
            pl.ds(pl.multiple_of(me * rows_out, SUB), rows_out), :
        ]
        drain(got.at[1], out_ref.at[:, pl.ds(0, (n - 1) * LANES)])
        drain(sent.at[9], out_ref.at[:, pl.ds(0, (n - keep - 1) * LANES)])

    @pl.when(me < keep)
    def _():
        drain(sent.at[9], out_ref.at[:, pl.ds(0, (n - keep) * LANES)])

    drain(sent.at[2], far[0].at[0, pl.ds(0, (n - 1) * deep), :])
    drain(sent.at[3], inbox0)
    for p in range(2):

        @pl.when(parity != p)
        def _():
            drain(sent.at[4 + p], inbox1.at[pl.ds(0, len(range(p, LOCAL, 2)))])

    @pl.when(me > 0)
    def _():
        drain(sent.at[0], series[0].at[:, pl.ds(0, SUB * (LOCAL + 1)), :])


def kernel_body(n, intensity, cycle_label, valid_mask):
    frames, pixels = intensity.shape
    f32 = jnp.float32
    dma = pltpu.SemaphoreType.DMA
    scratch = [
        pltpu.VMEM((frames, pixels), f32),
        pltpu.VMEM((pixels // 256, 2 * Q, 256), jnp.bfloat16),
        pltpu.VMEM((1, pixels), jnp.int32),
        pltpu.VMEM((1, pixels), jnp.int32),
    ]
    scratch += [pltpu.VMEM((n, (frames >> l) + 2 * SUB, LANES), f32) for l in range(LOCAL)]
    scratch += [pltpu.VMEM((n, frames >> LOCAL, LANES), f32)]
    scratch += [
        pltpu.VMEM((1, (n * frames >> l) + 2 * SUB, LANES), f32) for l in range(LOCAL, LEVELS)
    ]
    scratch += [
        pltpu.VMEM((n, LOCAL * LAGS, SUB, LANES), f32),
        pltpu.VMEM((2, LOCAL, n, SUB, LANES), f32),
        pltpu.VMEM((LOCAL, n, SUB, LANES), f32),
        pltpu.VMEM(((LOCAL + 1) // 2, n, SUB, LANES), f32),
        pltpu.VMEM((LEVELS // 2, n, SUB, LANES), f32),
        pltpu.VMEM((LEVELS * LAGS, LANES), f32),
        dma((pixels // 256 + 2,)),
        dma((LOCAL,)),
        dma((sum(CHUNKS),)),
        dma((sum(CHUNKS),)),
        dma((max(CHUNKS),)),
        dma((10,)),
        dma((2,)),
    ]
    vmem = pl.BlockSpec(memory_space=pltpu.VMEM)
    return pl.pallas_call(
        functools.partial(kernel, n, frames),
        out_shape=pltpu.VMEM((LEVELS * LAGS // n, pixels), f32),
        in_specs=[pl.BlockSpec(memory_space=pl.ANY)] * 3,
        out_specs=vmem,
        scratch_shapes=scratch,
        compiler_params=pltpu.CompilerParams(collective_id=0, has_side_effects=True),
        name="multitau",
    )(intensity, cycle_label.reshape(1, pixels), valid_mask.reshape(1, pixels))


def route(intensity, cycle_label, valid_mask):
    n = lax.axis_size("tm")
    frames, pixels = intensity.shape
    fits = (
        lax.axis_size("pix") == 1
        and pixels == n * LANES
        and frames % (SUB << LOCAL) == 0
        and frames >> LOCAL >= 2 * SUB
        and LEVELS * LAGS == n * SUB
    )
    if fits:
        return kernel_body(n, intensity, cycle_label, valid_mask)
    return body(intensity, cycle_label, valid_mask)


def solution(mesh):
    placed = (P("tm", ("runs", "pix")), P(("runs", "pix")), P(("runs", "pix")))
    return jax.shard_map(
        route, mesh=mesh, in_specs=placed, out_specs=P("tm", ("runs", "pix")), check_vma=False
    )
```

```python
import functools
import jax
import jax.numpy as jnp
from jax import lax
from jax.experimental import pallas as pl
from jax.experimental.pallas import tpu as pltpu
from jax.sharding import PartitionSpec as P

Q = 128
LEVELS = 8
LAGS = 16


def coarsen(series):
    paired = series.reshape(series.shape[0] // 2, 2, series.shape[1])
    return (paired[:, 0] + paired[:, 1]) * 0.5


def level_rows(series, extension, total_frames):
    frames_here = series.shape[0]
    row_list = []
    for offset in range(extension.shape[0] + 1):
        inside = min(offset, frames_here)
        total = jnp.sum(series[: frames_here - inside] * series[inside:], axis=0)
        if offset > 0:
            tail_rows = series[frames_here - inside :]
            total = total + jnp.sum(tail_rows * extension[offset - inside : offset], axis=0)
        row_list.append(total / (total_frames - offset))
    return row_list


def pixel_rows(gathered):
    series = gathered[:, 0, :]
    row_list = []
    for height in range(LEVELS):
        if height > 0:
            series = coarsen(series)
        extension = jnp.zeros((LAGS - 1, series.shape[1]), jnp.float32)
        row_list = row_list + level_rows(series, extension, series.shape[0])
    return jnp.stack(row_list)


def body(intensity, cycle_label, valid_mask):
    valid_flag = valid_mask.astype(jnp.float32)
    member = (cycle_label[:, None] == jnp.arange(Q, dtype=jnp.int32)[None, :]).astype(jnp.float32)
    weighted = member * valid_flag[:, None]
    partial_sum = jnp.dot(intensity, weighted, precision=lax.Precision.HIGHEST)
    partial_count = jnp.sum(weighted, axis=0)
    cycle_sum, cycle_count = lax.psum((partial_sum, partial_count), "pix")
    cycle_mean = cycle_sum / cycle_count[None, :]
    per_pixel = lax.dot_general(
        cycle_mean, member, (((1,), (1,)), ((), ())), precision=lax.Precision.HIGHEST
    )
    normed = valid_flag[None, :] * intensity / per_pixel
    devices_tm = lax.axis_size("tm")
    tile_width = normed.shape[1] // devices_tm
    pieces = normed.reshape(normed.shape[0], devices_tm, tile_width)
    rows_local = pixel_rows(lax.all_to_all(pieces, "tm", split_axis=1, concat_axis=0, tiled=True))
    return lax.all_to_all(rows_local, "tm", split_axis=0, concat_axis=1, tiled=True)

LOCAL = 3
CHUNKS = (4, 4, 1)
LANES = 128
SUB = 8
HALO = 2 * SUB
UNROLL = 4


def split(x):
    high = x.astype(jnp.bfloat16)
    return high, (x - high.astype(jnp.float32)).astype(jnp.bfloat16)


def fold_rows(parts):
    row = lax.broadcasted_iota(jnp.int32, (SUB, LANES), 0)
    for step in (4, 2, 1):
        keep = (row & step) == 0

        def swap(v, step=step, keep=keep):
            if step == 4:
                return pltpu.roll(v, 4, 0)
            return jnp.where(keep, pltpu.roll(v, SUB - step, 0), pltpu.roll(v, step, 0))

        parts = [
            jnp.where(keep, parts[i], parts[i + step]) + swap(jnp.where(keep, parts[i + step], parts[i]))
            for i in range(step)
        ]
    return parts[0]


def add_lags(ref, c, blocks, sums, first=0, sign=1):
    for b in blocks:
        base = ref[c, pl.ds(first + b * SUB, SUB), :]
        for k in range(LAGS):
            term = base * ref[c, pl.ds(first + b * SUB + sign * k, SUB), :]
            sums[k] = term if sums[k] is None else sums[k] + term
    return sums


def each(first, last, step):
    width = UNROLL
    while (last - first) % width:
        width //= 2

    def several(i, carry):
        for k in range(width):
            step(first + i * width + k, carry)
        return carry

    lax.fori_loop(0, (last - first) // width, several, 0)


def halve(ref, c, start, count):
    even = ref[c, pl.ds(start, count, stride=2), :]
    odd = ref[c, pl.ds(start + 1, count, stride=2), :]
    return (even + odd) * 0.5


def kernel(n, frames, x_hbm, lab_hbm, val_hbm, out_ref, *scratch):
    it = iter(scratch)
    x, wt, lab_ref, val_ref = (next(it) for _ in range(4))
    series = [next(it) for _ in range(LOCAL + 1)]
    far = [next(it) for _ in range(LEVELS - LOCAL)]
    keepers, partial, inbox0, inbox1, inbox, result = (next(it) for _ in range(6))
    load_sem, halo_recv, core_recv, pair_recv, plane_recv, sent, got = (next(it) for _ in range(7))
    me = lax.axis_index("tm")
    rows_out = LEVELS * LAGS // n
    total = n * frames
    groups = x.shape[1] // 256
    keep = LOCAL * LAGS // rows_out
    chip = LAGS // rows_out
    stack = 2 * chip
    planes = n // stack
    side, parity, plane = lax.rem(me, chip), lax.rem(me // chip, 2), me // stack

    loads = [
        pltpu.make_async_copy(
            x_hbm.at[:, pl.ds(g * 256, 256)], x.at[:, pl.ds(g * 256, 256)], load_sem.at[g]
        )
        for g in range(groups)
    ]
    lists = [
        pltpu.make_async_copy(lab_hbm, lab_ref, load_sem.at[groups]),
        pltpu.make_async_copy(val_hbm, val_ref, load_sem.at[groups + 1]),
    ]
    for copy in lists + loads:
        copy.start()

    barrier = pltpu.get_barrier_semaphore()

    @pl.loop(1, n)
    def _(d):
        pl.semaphore_signal(
            barrier, inc=1, device_id={"tm": lax.rem(me + d, n)}, device_id_type=pl.DeviceIdType.MESH
        )

    def remote(src, dst, send_sem, recv_sem, target):
        return pltpu.make_async_remote_copy(
            src_ref=src,
            dst_ref=dst,
            send_sem=send_sem,
            recv_sem=recv_sem,
            device_id={"tm": target},
            device_id_type=pl.DeviceIdType.MESH,
        )

    def drain(sem, ref):
        pltpu.make_async_copy(ref, ref, sem).wait()

    after = lax.rem(me + 1, n)

    for copy in lists:
        copy.wait()
    cycle = lax.broadcasted_iota(jnp.int32, (Q, 256), 0)
    members = jnp.zeros((Q, 256), jnp.float32)
    for g in range(groups):
        lab = lab_ref[:, pl.ds(g * 256, 256)]
        val = val_ref[:, pl.ds(g * 256, 256)].astype(jnp.float32)
        member = jnp.where(lab == cycle, val, 0.0)
        members = members + member
        wt[g] = jnp.concatenate([member.astype(jnp.bfloat16)] * 2, axis=0)

    acc = jnp.zeros((Q, 2 * frames), jnp.float32)
    for g in range(groups):
        loads[g].wait()
        rhs = jnp.concatenate(split(x[:, pl.ds(g * 256, 256)]), axis=0)
        acc = acc + lax.dot_general(
            wt[g, pl.ds(0, Q)], rhs, (((1,), (1,)), ((), ())), preferred_element_type=jnp.float32
        )
    count = jnp.sum(members, axis=1, keepdims=True)
    inverse = (count / (acc[:, :frames] + acc[:, frames:])).T

    def normalise(first, count):
        lhs = jnp.concatenate(split(inverse[first : first + count]), axis=1)
        for g in range(groups):
            scale = jnp.dot(lhs, wt[g], preferred_element_type=jnp.float32)
            normed = x[pl.ds(first, count), pl.ds(g * 256, 256)] * scale
            series[0][2 * g, pl.ds(HALO + first, count), :] = normed[:, :LANES]
            series[0][2 * g + 1, pl.ds(HALO + first, count), :] = normed[:, LANES:]

    def halo(l):
        count = HALO if l == 0 else SUB
        return remote(
            series[l].at[:, pl.ds(frames >> l, count), :],
            series[l].at[:, pl.ds(0, count), :],
            sent.at[0],
            halo_recv.at[l],
            after,
        )

    normalise(frames - HALO, HALO)
    pl.semaphore_wait(barrier, n - 1)

    @pl.when(me < n - 1)
    def _():
        halo(0).start()

    normalise(0, frames - HALO)

    def coarse(c, carry):
        for l in range(1, LOCAL + 1):
            series[l][c, pl.ds(0 if l == LOCAL else HALO, frames >> l), :] = halve(
                series[l - 1], c, HALO, frames >> l
            )
        return carry

    each(0, n, coarse)

    @pl.when(me < n - 1)
    def _():
        for l in range(1, LOCAL):
            halo(l).start()

    deep = frames >> LOCAL

    def spread():
        @pl.loop(1, n)
        def _(d):
            peer = lax.rem(me + d, n)
            remote(
                series[LOCAL].at[peer],
                far[0].at[0, pl.ds(pl.multiple_of(me * deep, SUB), deep), :],
                sent.at[2],
                got.at[0],
                peer,
            ).start()

    def inside(l):
        def one(c, carry):
            blocks = range(2, (frames >> l) // SUB)
            sums = add_lags(series[l], c, blocks, [None] * LAGS, HALO, -1)
            for k in range(LAGS):
                keepers[c, l * LAGS + k] = sums[k]
            return carry

        each(0, n, one)

    inside(0)

    @pl.when(me == 0)
    def _():
        for l in range(LOCAL):
            count = HALO if l == 0 else SUB
            series[l][:, pl.ds(0, count), :] = jnp.zeros((n, count, LANES), jnp.float32)

    def parts(l, q):
        block = n // CHUNKS[l]
        return pl.ds(q * block, block)

    def sem(l, q):
        return sum(CHUNKS[:l]) + q

    def to_core(l, q):
        part = parts(l, q)
        return remote(
            partial.at[1 - side, l, part],
            inbox0.at[l, part],
            sent.at[3],
            core_recv.at[sem(l, q)],
            me + 1 - 2 * side,
        )

    def to_pair(l, q):
        part = parts(l, q)
        return remote(
            partial.at[side, l, part],
            inbox1.at[l // 2, part],
            sent.at[4 + l % 2],
            pair_recv.at[sem(l, q)],
            me + chip - 2 * chip * parity,
        )

    def half(y):
        return pl.ds(y * (n // 2), n // 2)

    def to_half():
        part = half(1 - parity)
        return remote(
            partial.at[side, 2, part],
            inbox1.at[1, part],
            sent.at[1],
            pair_recv.at[sem(2, 0)],
            me + chip - 2 * chip * parity,
        )

    def to_middle():
        part = half(parity)
        return remote(
            partial.at[side, 2, part], inbox.at[plane, part], sent.at[8], plane_recv.at[0], stack + side
        )

    def to_plane(l, q):
        part = parts(l, q)
        return remote(
            partial.at[side, l, part],
            inbox.at[plane, part],
            sent.at[6 + l],
            plane_recv.at[q],
            lax.rem(me, stack) + (l // 2) * stack,
        )

    def edges(l, q):
        block = n // CHUNKS[l]

        def edge(c, carry):
            if l > 0:
                series[l][c, pl.ds(SUB, SUB), :] = halve(series[l - 1], c, 0, SUB)
            sums = [keepers[c, l * LAGS + k] for k in range(LAGS)]
            sums = add_lags(series[l], c, range(2), sums, HALO, -1)
            for h in range(LAGS // SUB):
                partial[h, l, c] = fold_rows(sums[h * SUB : (h + 1) * SUB])
            return carry

        each(q * block, (q + 1) * block, edge)

    def compute(l):
        if l > 0:
            inside(l)

        @pl.when(me > 0)
        def _():
            drain(halo_recv.at[l], series[l].at[:, pl.ds(0, 2 * SUB if l == 0 else SUB), :])

        for q in range(CHUNKS[l]):
            edges(l, q)
            to_core(l, q).start()

    def across(l):
        for q in range(CHUNKS[l]):
            part = parts(l, q)
            to_core(l, q).wait_recv()
            partial[side, l, part] = partial[side, l, part] + inbox0[l, part]

            @pl.when(parity != l % 2)
            def _():
                to_pair(l, q).start()

    def along(l):
        for q in range(CHUNKS[l]):

            @pl.when(parity == l % 2)
            def _():
                part = parts(l, q)
                to_pair(l, q).wait_recv()
                partial[side, l, part] = partial[side, l, part] + inbox1[l // 2, part]

                @pl.when(plane != l // 2)
                def _():
                    to_plane(l, q).start()

    compute(0)
    spread()
    compute(1)
    across(0)
    across(1)
    compute(2)
    to_core(2, 0).wait_recv()
    partial[side, 2] = partial[side, 2] + inbox0[2]
    to_half().start()
    along(0)
    along(1)
    to_half().wait_recv()
    partial[side, 2, half(parity)] = partial[side, 2, half(parity)] + inbox1[1, half(parity)]

    @pl.when((plane != 1) | (parity != 0))
    def _():
        to_middle().start()

    far[0][0, pl.ds(pl.multiple_of(me * deep, SUB), deep), :] = series[LOCAL][me]
    for i in range(LEVELS - LOCAL):
        count = total >> (LOCAL + i)
        far[i][0, pl.ds(count, 2 * SUB), :] = jnp.zeros((2 * SUB, LANES), jnp.float32)
    drain(got.at[0], far[0].at[0, pl.ds(0, (n - 1) * deep), :])
    lag = lax.broadcasted_iota(jnp.int32, (SUB, LANES), 0)

    def weight(l, h):
        return 1.0 / ((total >> l) - h * SUB - lag).astype(jnp.float32)

    for i in range(LEVELS - LOCAL):
        l = LOCAL + i
        count = total >> l
        if i > 0:
            far[i][0, pl.ds(0, count), :] = halve(far[i - 1], 0, 0, count)
        sums = add_lags(far[i], 0, range(count // SUB), [None] * LAGS)
        for h in range(LAGS // SUB):
            result[pl.ds(l * LAGS + h * SUB, SUB), :] = fold_rows(
                sums[h * SUB : (h + 1) * SUB]
            ) * weight(l, h)

    @pl.loop(1, n)
    def _(d):
        peer = lax.rem(me + d, n)

        @pl.when(peer >= keep)
        def _():
            remote(
                result.at[pl.ds(pl.multiple_of(peer * rows_out, SUB), rows_out), :],
                out_ref.at[:, pl.ds(pl.multiple_of(me * LANES, LANES), LANES)],
                sent.at[9],
                got.at[1],
                peer,
            ).start()


    @pl.when((plane == 1) & (parity == 0))
    def _():
        scale = 1.0 / ((total >> 2) - side * SUB - lag).astype(jnp.float32)
        drain(plane_recv.at[0], keepers.at[pl.ds(0, ((planes - 1) * n + n // 2) // SUB), pl.ds(0, SUB)])
        for c in range(n):
            rows = partial[side, 2, c] if c < n // 2 else inbox[1, c]
            for source in range(planes):
                if source != 1:
                    rows = rows + inbox[source, c]
            out_ref[:, pl.ds(c * LANES, LANES)] = rows * scale

    @pl.when((plane != 1) | (parity != 0))
    def _():
        drain(sent.at[8], inbox.at[0, pl.ds(0, n // 2)])

    for l in range(2):

        @pl.when((plane == l // 2) & (parity == l % 2))
        def _():
            scale = 1.0 / ((total >> l) - side * SUB - lag).astype(jnp.float32)
            for q in range(CHUNKS[l]):
                block = n // CHUNKS[l]
                drain(plane_recv.at[q], inbox.at[pl.ds(0, planes - 1), pl.ds(q * block, block)])
                for c in range(q * block, (q + 1) * block):
                    rows = partial[side, l, c]
                    for source in range(planes):
                        if source != l // 2:
                            rows = rows + inbox[source, c]
                    out_ref[:, pl.ds(c * LANES, LANES)] = rows * scale

        @pl.when((plane != l // 2) & (parity == l % 2))
        def _():
            drain(sent.at[6 + l], inbox.at[0])

    @pl.when(me >= keep)
    def _():
        out_ref[:, pl.ds(pl.multiple_of(me * LANES, LANES), LANES)] = result[
            pl.ds(pl.multiple_of(me * rows_out, SUB), rows_out), :
        ]
        drain(got.at[1], out_ref.at[:, pl.ds(0, (n - 1) * LANES)])
        drain(sent.at[9], out_ref.at[:, pl.ds(0, (n - keep - 1) * LANES)])

    @pl.when(me < keep)
    def _():
        drain(sent.at[9], out_ref.at[:, pl.ds(0, (n - keep) * LANES)])

    drain(sent.at[2], far[0].at[0, pl.ds(0, (n - 1) * deep), :])
    drain(sent.at[3], inbox0)
    drain(sent.at[1], inbox1.at[1, pl.ds(0, n // 2)])
    for p in range(2):

        @pl.when(parity != p)
        def _():
            drain(sent.at[4 + p], inbox1.at[0])

    @pl.when(me < n - 1)
    def _():
        drain(sent.at[0], series[0].at[:, pl.ds(0, SUB * (LOCAL + 1)), :])


def kernel_body(n, intensity, cycle_label, valid_mask):
    frames, pixels = intensity.shape
    f32 = jnp.float32
    dma = pltpu.SemaphoreType.DMA
    scratch = [
        pltpu.VMEM((frames, pixels), f32),
        pltpu.VMEM((pixels // 256, 2 * Q, 256), jnp.bfloat16),
        pltpu.VMEM((1, pixels), jnp.int32),
        pltpu.VMEM((1, pixels), jnp.int32),
    ]
    scratch += [pltpu.VMEM((n, (frames >> l) + 2 * SUB, LANES), f32) for l in range(LOCAL)]
    scratch += [pltpu.VMEM((n, frames >> LOCAL, LANES), f32)]
    scratch += [
        pltpu.VMEM((1, (n * frames >> l) + 2 * SUB, LANES), f32) for l in range(LOCAL, LEVELS)
    ]
    scratch += [
        pltpu.VMEM((n, LOCAL * LAGS, SUB, LANES), f32),
        pltpu.VMEM((2, LOCAL, n, SUB, LANES), f32),
        pltpu.VMEM((LOCAL, n, SUB, LANES), f32),
        pltpu.VMEM(((LOCAL + 1) // 2, n, SUB, LANES), f32),
        pltpu.VMEM((LEVELS // 2, n, SUB, LANES), f32),
        pltpu.VMEM((LEVELS * LAGS, LANES), f32),
        dma((pixels // 256 + 2,)),
        dma((LOCAL,)),
        dma((sum(CHUNKS),)),
        dma((sum(CHUNKS),)),
        dma((max(CHUNKS),)),
        dma((10,)),
        dma((2,)),
    ]
    vmem = pl.BlockSpec(memory_space=pltpu.VMEM)
    return pl.pallas_call(
        functools.partial(kernel, n, frames),
        out_shape=pltpu.VMEM((LEVELS * LAGS // n, pixels), f32),
        in_specs=[pl.BlockSpec(memory_space=pl.ANY)] * 3,
        out_specs=vmem,
        scratch_shapes=scratch,
        compiler_params=pltpu.CompilerParams(collective_id=0, has_side_effects=True),
        name="multitau",
    )(intensity, cycle_label.reshape(1, pixels), valid_mask.reshape(1, pixels))


def route(intensity, cycle_label, valid_mask):
    n = lax.axis_size("tm")
    frames, pixels = intensity.shape
    fits = (
        lax.axis_size("pix") == 1
        and pixels == n * LANES
        and frames % (SUB << LOCAL) == 0
        and frames >> LOCAL >= 2 * SUB
        and LEVELS * LAGS == n * SUB
    )
    if fits:
        return kernel_body(n, intensity, cycle_label, valid_mask)
    return body(intensity, cycle_label, valid_mask)


def solution(mesh):
    placed = (P("tm", ("runs", "pix")), P(("runs", "pix")), P(("runs", "pix")))
    return jax.shard_map(
        route, mesh=mesh, in_specs=placed, out_specs=P("tm", ("runs", "pix")), check_vma=False
    )
```

```python
import functools
import jax
import jax.numpy as jnp
from jax import lax
from jax.experimental import pallas as pl
from jax.experimental.pallas import tpu as pltpu
from jax.sharding import PartitionSpec as P

Q = 128
LEVELS = 8
LAGS = 16


def coarsen(series):
    paired = series.reshape(series.shape[0] // 2, 2, series.shape[1])
    return (paired[:, 0] + paired[:, 1]) * 0.5


def level_rows(series, extension, total_frames):
    frames_here = series.shape[0]
    row_list = []
    for offset in range(extension.shape[0] + 1):
        inside = min(offset, frames_here)
        total = jnp.sum(series[: frames_here - inside] * series[inside:], axis=0)
        if offset > 0:
            tail_rows = series[frames_here - inside :]
            total = total + jnp.sum(tail_rows * extension[offset - inside : offset], axis=0)
        row_list.append(total / (total_frames - offset))
    return row_list


def pixel_rows(gathered):
    series = gathered[:, 0, :]
    row_list = []
    for height in range(LEVELS):
        if height > 0:
            series = coarsen(series)
        extension = jnp.zeros((LAGS - 1, series.shape[1]), jnp.float32)
        row_list = row_list + level_rows(series, extension, series.shape[0])
    return jnp.stack(row_list)


def body(intensity, cycle_label, valid_mask):
    valid_flag = valid_mask.astype(jnp.float32)
    member = (cycle_label[:, None] == jnp.arange(Q, dtype=jnp.int32)[None, :]).astype(jnp.float32)
    weighted = member * valid_flag[:, None]
    partial_sum = jnp.dot(intensity, weighted, precision=lax.Precision.HIGHEST)
    partial_count = jnp.sum(weighted, axis=0)
    cycle_sum, cycle_count = lax.psum((partial_sum, partial_count), "pix")
    cycle_mean = cycle_sum / cycle_count[None, :]
    per_pixel = lax.dot_general(
        cycle_mean, member, (((1,), (1,)), ((), ())), precision=lax.Precision.HIGHEST
    )
    normed = valid_flag[None, :] * intensity / per_pixel
    devices_tm = lax.axis_size("tm")
    tile_width = normed.shape[1] // devices_tm
    pieces = normed.reshape(normed.shape[0], devices_tm, tile_width)
    rows_local = pixel_rows(lax.all_to_all(pieces, "tm", split_axis=1, concat_axis=0, tiled=True))
    return lax.all_to_all(rows_local, "tm", split_axis=0, concat_axis=1, tiled=True)

LOCAL = 3
CHUNKS = (4, 4, 1)
HALOS = (4, 2, 1)
LANES = 128
SUB = 8
HALO = 2 * SUB
UNROLL = 4


def split(x):
    high = x.astype(jnp.bfloat16)
    return high, (x - high.astype(jnp.float32)).astype(jnp.bfloat16)


def fold_rows(parts):
    row = lax.broadcasted_iota(jnp.int32, (SUB, LANES), 0)
    for step in (4, 2, 1):
        keep = (row & step) == 0

        def swap(v, step=step, keep=keep):
            if step == 4:
                return pltpu.roll(v, 4, 0)
            return jnp.where(keep, pltpu.roll(v, SUB - step, 0), pltpu.roll(v, step, 0))

        parts = [
            jnp.where(keep, parts[i], parts[i + step]) + swap(jnp.where(keep, parts[i + step], parts[i]))
            for i in range(step)
        ]
    return parts[0]


def add_lags(ref, c, blocks, sums, first=0, sign=1):
    for b in blocks:
        base = ref[c, pl.ds(first + b * SUB, SUB), :]
        for k in range(LAGS):
            term = base * ref[c, pl.ds(first + b * SUB + sign * k, SUB), :]
            sums[k] = term if sums[k] is None else sums[k] + term
    return sums


def each(first, last, step):
    width = UNROLL
    while (last - first) % width:
        width //= 2

    def several(i, carry):
        for k in range(width):
            step(first + i * width + k, carry)
        return carry

    lax.fori_loop(0, (last - first) // width, several, 0)


def halve(ref, c, start, count):
    even = ref[c, pl.ds(start, count, stride=2), :]
    odd = ref[c, pl.ds(start + 1, count, stride=2), :]
    return (even + odd) * 0.5


def kernel(n, frames, x_hbm, lab_hbm, val_hbm, out_ref, *scratch):
    it = iter(scratch)
    x, wt, lab_ref, val_ref = (next(it) for _ in range(4))
    series = [next(it) for _ in range(LOCAL + 1)]
    far = [next(it) for _ in range(LEVELS - LOCAL)]
    keepers, partial, inbox0, inbox1, inbox, result = (next(it) for _ in range(6))
    load_sem, halo_recv, core_recv, pair_recv, plane_recv, sent, got = (next(it) for _ in range(7))
    me = lax.axis_index("tm")
    rows_out = LEVELS * LAGS // n
    total = n * frames
    groups = x.shape[1] // 256
    keep = LOCAL * LAGS // rows_out
    chip = LAGS // rows_out
    stack = 2 * chip
    planes = n // stack
    side, parity, plane = lax.rem(me, chip), lax.rem(me // chip, 2), me // stack

    half_width = x.shape[1] // 2
    loads = [
        pltpu.make_async_copy(
            x_hbm.at[:, pl.ds(g * half_width, half_width)],
            x.at[:, pl.ds(g * half_width, half_width)],
            load_sem.at[g],
        )
        for g in range(2)
    ]
    lists = [
        pltpu.make_async_copy(lab_hbm, lab_ref, load_sem.at[2]),
        pltpu.make_async_copy(val_hbm, val_ref, load_sem.at[3]),
    ]
    for copy in lists + loads:
        copy.start()

    barrier = pltpu.get_barrier_semaphore()

    @pl.loop(1, n)
    def _(d):
        pl.semaphore_signal(
            barrier, inc=1, device_id={"tm": lax.rem(me + d, n)}, device_id_type=pl.DeviceIdType.MESH
        )

    def remote(src, dst, send_sem, recv_sem, target):
        return pltpu.make_async_remote_copy(
            src_ref=src,
            dst_ref=dst,
            send_sem=send_sem,
            recv_sem=recv_sem,
            device_id={"tm": target},
            device_id_type=pl.DeviceIdType.MESH,
        )

    def drain(sem, ref):
        pltpu.make_async_copy(ref, ref, sem).wait()

    after = lax.rem(me + 1, n)

    for copy in lists:
        copy.wait()
    cycle = lax.broadcasted_iota(jnp.int32, (Q, 256), 0)
    members = jnp.zeros((Q, 256), jnp.float32)
    for g in range(groups):
        lab = lab_ref[:, pl.ds(g * 256, 256)]
        val = val_ref[:, pl.ds(g * 256, 256)].astype(jnp.float32)
        member = jnp.where(lab == cycle, val, 0.0)
        members = members + member
        wt[g] = jnp.concatenate([member.astype(jnp.bfloat16)] * 2, axis=0)

    acc = jnp.zeros((Q, 2 * frames), jnp.float32)
    for g in range(groups):
        if g % (groups // 2) == 0:
            loads[g * 2 // groups].wait()
        rhs = jnp.concatenate(split(x[:, pl.ds(g * 256, 256)]), axis=0)
        acc = acc + lax.dot_general(
            wt[g, pl.ds(0, Q)], rhs, (((1,), (1,)), ((), ())), preferred_element_type=jnp.float32
        )
    count = jnp.sum(members, axis=1, keepdims=True)
    inverse = (count / (acc[:, :frames] + acc[:, frames:])).T

    def normalise(first, count):
        lhs = jnp.concatenate(split(inverse[first : first + count]), axis=1)
        for g in range(groups):
            scale = jnp.dot(lhs, wt[g], preferred_element_type=jnp.float32)
            normed = x[pl.ds(first, count), pl.ds(g * 256, 256)] * scale
            series[0][2 * g, pl.ds(HALO + first, count), :] = normed[:, :LANES]
            series[0][2 * g + 1, pl.ds(HALO + first, count), :] = normed[:, LANES:]

    def halo(l, q):
        count = HALO if l == 0 else SUB
        part = pl.ds(q * (n // HALOS[l]), n // HALOS[l])
        return remote(
            series[l].at[part, pl.ds(frames >> l, count), :],
            series[l].at[part, pl.ds(0, count), :],
            sent.at[0],
            halo_recv.at[sum(HALOS[:l]) + q],
            after,
        )

    normalise(frames - HALO, HALO)
    pl.semaphore_wait(barrier, n - 1)

    @pl.when(me < n - 1)
    def _():
        for q in range(HALOS[0]):
            halo(0, q).start()

    normalise(0, frames - HALO)

    def coarse(c, carry):
        for l in range(1, LOCAL + 1):
            series[l][c, pl.ds(0 if l == LOCAL else HALO, frames >> l), :] = halve(
                series[l - 1], c, HALO, frames >> l
            )
        return carry

    each(0, n, coarse)

    @pl.when(me < n - 1)
    def _():
        for l in range(1, LOCAL):
            for q in range(HALOS[l]):
                halo(l, q).start()

    deep = frames >> LOCAL

    def spread():
        @pl.loop(1, n)
        def _(d):
            peer = lax.rem(me + d, n)
            remote(
                series[LOCAL].at[peer],
                far[0].at[0, pl.ds(pl.multiple_of(me * deep, SUB), deep), :],
                sent.at[2],
                got.at[0],
                peer,
            ).start()

    def inside(l):
        def one(c, carry):
            blocks = range(2, (frames >> l) // SUB)
            sums = add_lags(series[l], c, blocks, [None] * LAGS, HALO, -1)
            for k in range(LAGS):
                keepers[c, l * LAGS + k] = sums[k]
            return carry

        each(0, n, one)

    inside(0)

    @pl.when(me == 0)
    def _():
        for l in range(LOCAL):
            count = HALO if l == 0 else SUB
            series[l][:, pl.ds(0, count), :] = jnp.zeros((n, count, LANES), jnp.float32)

    def parts(l, q):
        block = n // CHUNKS[l]
        return pl.ds(q * block, block)

    def sem(l, q):
        return sum(CHUNKS[:l]) + q

    def to_core(l, q):
        part = parts(l, q)
        return remote(
            partial.at[1 - side, l, part],
            inbox0.at[l, part],
            sent.at[3],
            core_recv.at[sem(l, q)],
            me + 1 - 2 * side,
        )

    def to_pair(l, q):
        part = parts(l, q)
        return remote(
            partial.at[side, l, part],
            inbox1.at[l // 2, part],
            sent.at[4 + l % 2],
            pair_recv.at[sem(l, q)],
            me + chip - 2 * chip * parity,
        )

    def half(y):
        return pl.ds(y * (n // 2), n // 2)

    def to_half():
        part = half(1 - parity)
        return remote(
            partial.at[side, 2, part],
            inbox1.at[1, part],
            sent.at[1],
            pair_recv.at[sem(2, 0)],
            me + chip - 2 * chip * parity,
        )

    def to_middle():
        part = half(parity)
        return remote(
            partial.at[side, 2, part], inbox.at[plane, part], sent.at[8], plane_recv.at[0], stack + side
        )

    def to_plane(l, q):
        part = parts(l, q)
        return remote(
            partial.at[side, l, part],
            inbox.at[plane, part],
            sent.at[6 + l],
            plane_recv.at[q],
            lax.rem(me, stack) + (l // 2) * stack,
        )

    def edges(l, q):
        block = n // CHUNKS[l]

        def edge(c, carry):
            if l > 0:
                series[l][c, pl.ds(SUB, SUB), :] = halve(series[l - 1], c, 0, SUB)
            sums = [keepers[c, l * LAGS + k] for k in range(LAGS)]
            sums = add_lags(series[l], c, range(2), sums, HALO, -1)
            for h in range(LAGS // SUB):
                partial[h, l, c] = fold_rows(sums[h * SUB : (h + 1) * SUB])
            return carry

        each(q * block, (q + 1) * block, edge)

    def compute(l):
        if l > 0:
            inside(l)

        for q in range(CHUNKS[l]):
            if q % (CHUNKS[l] // HALOS[l]) == 0:

                @pl.when(me > 0)
                def _():
                    halo(l, q * HALOS[l] // CHUNKS[l]).wait_recv()

            edges(l, q)
            to_core(l, q).start()

    def across(l):
        for q in range(CHUNKS[l]):
            part = parts(l, q)
            to_core(l, q).wait_recv()
            partial[side, l, part] = partial[side, l, part] + inbox0[l, part]

            @pl.when(parity != l % 2)
            def _():
                to_pair(l, q).start()

    def along(l):
        for q in range(CHUNKS[l]):

            @pl.when(parity == l % 2)
            def _():
                part = parts(l, q)
                to_pair(l, q).wait_recv()
                partial[side, l, part] = partial[side, l, part] + inbox1[l // 2, part]

                @pl.when(plane != l // 2)
                def _():
                    to_plane(l, q).start()

    compute(0)

    @pl.when(side == 0)
    def _():
        across(0)

    compute(1)
    spread()

    @pl.when(side > 0)
    def _():
        across(0)

    across(1)
    compute(2)
    to_core(2, 0).wait_recv()
    partial[side, 2] = partial[side, 2] + inbox0[2]
    to_half().start()
    along(0)
    along(1)
    to_half().wait_recv()
    partial[side, 2, half(parity)] = partial[side, 2, half(parity)] + inbox1[1, half(parity)]

    @pl.when((plane != 1) | (parity != 0))
    def _():
        to_middle().start()

    far[0][0, pl.ds(pl.multiple_of(me * deep, SUB), deep), :] = series[LOCAL][me]
    for i in range(LEVELS - LOCAL):
        count = total >> (LOCAL + i)
        far[i][0, pl.ds(count, 2 * SUB), :] = jnp.zeros((2 * SUB, LANES), jnp.float32)
    drain(got.at[0], far[0].at[0, pl.ds(0, (n - 1) * deep), :])
    lag = lax.broadcasted_iota(jnp.int32, (SUB, LANES), 0)

    def weight(l, h):
        return 1.0 / ((total >> l) - h * SUB - lag).astype(jnp.float32)

    for i in range(LEVELS - LOCAL):
        l = LOCAL + i
        count = total >> l
        if i > 0:
            far[i][0, pl.ds(0, count), :] = halve(far[i - 1], 0, 0, count)
        sums = add_lags(far[i], 0, range(count // SUB), [None] * LAGS)
        for h in range(LAGS // SUB):
            result[pl.ds(l * LAGS + h * SUB, SUB), :] = fold_rows(
                sums[h * SUB : (h + 1) * SUB]
            ) * weight(l, h)

    @pl.loop(1, n)
    def _(d):
        peer = lax.rem(me + d, n)

        @pl.when(peer >= keep)
        def _():
            remote(
                result.at[pl.ds(pl.multiple_of(peer * rows_out, SUB), rows_out), :],
                out_ref.at[:, pl.ds(pl.multiple_of(me * LANES, LANES), LANES)],
                sent.at[9],
                got.at[1],
                peer,
            ).start()


    @pl.when((plane == 1) & (parity == 0))
    def _():
        scale = 1.0 / ((total >> 2) - side * SUB - lag).astype(jnp.float32)
        drain(plane_recv.at[0], keepers.at[pl.ds(0, ((planes - 1) * n + n // 2) // SUB), pl.ds(0, SUB)])
        for c in range(n):
            rows = partial[side, 2, c] if c < n // 2 else inbox[1, c]
            for source in range(planes):
                if source != 1:
                    rows = rows + inbox[source, c]
            out_ref[:, pl.ds(c * LANES, LANES)] = rows * scale

    @pl.when((plane != 1) | (parity != 0))
    def _():
        drain(sent.at[8], inbox.at[0, pl.ds(0, n // 2)])

    for l in range(2):

        @pl.when((plane == l // 2) & (parity == l % 2))
        def _():
            scale = 1.0 / ((total >> l) - side * SUB - lag).astype(jnp.float32)
            for q in range(CHUNKS[l]):
                block = n // CHUNKS[l]
                drain(plane_recv.at[q], inbox.at[pl.ds(0, planes - 1), pl.ds(q * block, block)])
                for c in range(q * block, (q + 1) * block):
                    rows = partial[side, l, c]
                    for source in range(planes):
                        if source != l // 2:
                            rows = rows + inbox[source, c]
                    out_ref[:, pl.ds(c * LANES, LANES)] = rows * scale

        @pl.when((plane != l // 2) & (parity == l % 2))
        def _():
            drain(sent.at[6 + l], inbox.at[0])

    @pl.when(me >= keep)
    def _():
        out_ref[:, pl.ds(pl.multiple_of(me * LANES, LANES), LANES)] = result[
            pl.ds(pl.multiple_of(me * rows_out, SUB), rows_out), :
        ]
        drain(got.at[1], out_ref.at[:, pl.ds(0, (n - 1) * LANES)])
        drain(sent.at[9], out_ref.at[:, pl.ds(0, (n - keep - 1) * LANES)])

    @pl.when(me < keep)
    def _():
        drain(sent.at[9], out_ref.at[:, pl.ds(0, (n - keep) * LANES)])

    drain(sent.at[2], far[0].at[0, pl.ds(0, (n - 1) * deep), :])
    drain(sent.at[3], inbox0)
    drain(sent.at[1], inbox1.at[1, pl.ds(0, n // 2)])
    for p in range(2):

        @pl.when(parity != p)
        def _():
            drain(sent.at[4 + p], inbox1.at[0])

    @pl.when(me < n - 1)
    def _():
        drain(sent.at[0], series[0].at[:, pl.ds(0, SUB * (LOCAL + 1)), :])


def kernel_body(n, intensity, cycle_label, valid_mask):
    frames, pixels = intensity.shape
    f32 = jnp.float32
    dma = pltpu.SemaphoreType.DMA
    scratch = [
        pltpu.VMEM((frames, pixels), f32),
        pltpu.VMEM((pixels // 256, 2 * Q, 256), jnp.bfloat16),
        pltpu.VMEM((1, pixels), jnp.int32),
        pltpu.VMEM((1, pixels), jnp.int32),
    ]
    scratch += [pltpu.VMEM((n, (frames >> l) + 2 * SUB, LANES), f32) for l in range(LOCAL)]
    scratch += [pltpu.VMEM((n, frames >> LOCAL, LANES), f32)]
    scratch += [
        pltpu.VMEM((1, (n * frames >> l) + 2 * SUB, LANES), f32) for l in range(LOCAL, LEVELS)
    ]
    scratch += [
        pltpu.VMEM((n, LOCAL * LAGS, SUB, LANES), f32),
        pltpu.VMEM((2, LOCAL, n, SUB, LANES), f32),
        pltpu.VMEM((LOCAL, n, SUB, LANES), f32),
        pltpu.VMEM(((LOCAL + 1) // 2, n, SUB, LANES), f32),
        pltpu.VMEM((LEVELS // 2, n, SUB, LANES), f32),
        pltpu.VMEM((LEVELS * LAGS, LANES), f32),
        dma((4,)),
        dma((sum(HALOS),)),
        dma((sum(CHUNKS),)),
        dma((sum(CHUNKS),)),
        dma((max(CHUNKS),)),
        dma((10,)),
        dma((2,)),
    ]
    vmem = pl.BlockSpec(memory_space=pltpu.VMEM)
    return pl.pallas_call(
        functools.partial(kernel, n, frames),
        out_shape=pltpu.VMEM((LEVELS * LAGS // n, pixels), f32),
        in_specs=[pl.BlockSpec(memory_space=pl.ANY)] * 3,
        out_specs=vmem,
        scratch_shapes=scratch,
        compiler_params=pltpu.CompilerParams(collective_id=0, has_side_effects=True),
        name="multitau",
    )(intensity, cycle_label.reshape(1, pixels), valid_mask.reshape(1, pixels))


def route(intensity, cycle_label, valid_mask):
    n = lax.axis_size("tm")
    frames, pixels = intensity.shape
    fits = (
        lax.axis_size("pix") == 1
        and pixels == n * LANES
        and frames % (SUB << LOCAL) == 0
        and frames >> LOCAL >= 2 * SUB
        and LEVELS * LAGS == n * SUB
    )
    if fits:
        return kernel_body(n, intensity, cycle_label, valid_mask)
    return body(intensity, cycle_label, valid_mask)


def solution(mesh):
    placed = (P("tm", ("runs", "pix")), P(("runs", "pix")), P(("runs", "pix")))
    return jax.shard_map(
        route, mesh=mesh, in_specs=placed, out_specs=P("tm", ("runs", "pix")), check_vma=False
    )
```

```python
import functools
import jax
import jax.numpy as jnp
from jax import lax
from jax.experimental import pallas as pl
from jax.experimental.pallas import tpu as pltpu
from jax.sharding import PartitionSpec as P

Q = 128
LEVELS = 8
LAGS = 16


def coarsen(series):
    paired = series.reshape(series.shape[0] // 2, 2, series.shape[1])
    return (paired[:, 0] + paired[:, 1]) * 0.5


def level_rows(series, extension, total_frames):
    frames_here = series.shape[0]
    row_list = []
    for offset in range(extension.shape[0] + 1):
        inside = min(offset, frames_here)
        total = jnp.sum(series[: frames_here - inside] * series[inside:], axis=0)
        if offset > 0:
            tail_rows = series[frames_here - inside :]
            total = total + jnp.sum(tail_rows * extension[offset - inside : offset], axis=0)
        row_list.append(total / (total_frames - offset))
    return row_list


def pixel_rows(gathered):
    series = gathered[:, 0, :]
    row_list = []
    for height in range(LEVELS):
        if height > 0:
            series = coarsen(series)
        extension = jnp.zeros((LAGS - 1, series.shape[1]), jnp.float32)
        row_list = row_list + level_rows(series, extension, series.shape[0])
    return jnp.stack(row_list)


def body(intensity, cycle_label, valid_mask):
    valid_flag = valid_mask.astype(jnp.float32)
    member = (cycle_label[:, None] == jnp.arange(Q, dtype=jnp.int32)[None, :]).astype(jnp.float32)
    weighted = member * valid_flag[:, None]
    partial_sum = jnp.dot(intensity, weighted, precision=lax.Precision.HIGHEST)
    partial_count = jnp.sum(weighted, axis=0)
    cycle_sum, cycle_count = lax.psum((partial_sum, partial_count), "pix")
    cycle_mean = cycle_sum / cycle_count[None, :]
    per_pixel = lax.dot_general(
        cycle_mean, member, (((1,), (1,)), ((), ())), precision=lax.Precision.HIGHEST
    )
    normed = valid_flag[None, :] * intensity / per_pixel
    devices_tm = lax.axis_size("tm")
    tile_width = normed.shape[1] // devices_tm
    pieces = normed.reshape(normed.shape[0], devices_tm, tile_width)
    rows_local = pixel_rows(lax.all_to_all(pieces, "tm", split_axis=1, concat_axis=0, tiled=True))
    return lax.all_to_all(rows_local, "tm", split_axis=0, concat_axis=1, tiled=True)

LOCAL = 3
CHUNKS = (4, 4, 1)
HALOS = (4, 2, 1)
LANES = 128
SUB = 8
HALO = 2 * SUB
UNROLL = 4


def split(x):
    high = x.astype(jnp.bfloat16)
    return high, (x - high.astype(jnp.float32)).astype(jnp.bfloat16)


def fold_rows(parts):
    row = lax.broadcasted_iota(jnp.int32, (SUB, LANES), 0)
    for step in (4, 2, 1):
        keep = (row & step) == 0

        def swap(v, step=step, keep=keep):
            if step == 4:
                return pltpu.roll(v, 4, 0)
            return jnp.where(keep, pltpu.roll(v, SUB - step, 0), pltpu.roll(v, step, 0))

        parts = [
            jnp.where(keep, parts[i], parts[i + step]) + swap(jnp.where(keep, parts[i + step], parts[i]))
            for i in range(step)
        ]
    return parts[0]


def add_lags(ref, c, blocks, sums, first=0, sign=1):
    for b in blocks:
        base = ref[c, pl.ds(first + b * SUB, SUB), :]
        for k in range(LAGS):
            term = base * ref[c, pl.ds(first + b * SUB + sign * k, SUB), :]
            sums[k] = term if sums[k] is None else sums[k] + term
    return sums


def each(first, last, step):
    width = UNROLL
    while (last - first) % width:
        width //= 2

    def several(i, carry):
        for k in range(width):
            step(first + i * width + k, carry)
        return carry

    lax.fori_loop(0, (last - first) // width, several, 0)


def halve(ref, c, start, count):
    even = ref[c, pl.ds(start, count, stride=2), :]
    odd = ref[c, pl.ds(start + 1, count, stride=2), :]
    return (even + odd) * 0.5


def kernel(n, frames, x_hbm, lab_hbm, val_hbm, out_ref, *scratch):
    it = iter(scratch)
    x, wt, lab_ref, val_ref = (next(it) for _ in range(4))
    series = [next(it) for _ in range(LOCAL + 1)]
    far = [next(it) for _ in range(LEVELS - LOCAL)]
    keepers, partial, inbox0, inbox1, inbox, result = (next(it) for _ in range(6))
    load_sem, halo_recv, core_recv, pair_recv, plane_recv, sent, got = (next(it) for _ in range(7))
    me = lax.axis_index("tm")
    rows_out = LEVELS * LAGS // n
    total = n * frames
    groups = x.shape[1] // 256
    keep = LOCAL * LAGS // rows_out
    chip = LAGS // rows_out
    stack = 2 * chip
    planes = n // stack
    side, parity, plane = lax.rem(me, chip), lax.rem(me // chip, 2), me // stack

    half_width = x.shape[1] // 2
    loads = [
        pltpu.make_async_copy(
            x_hbm.at[:, pl.ds(g * half_width, half_width)],
            x.at[:, pl.ds(g * half_width, half_width)],
            load_sem.at[g],
        )
        for g in range(2)
    ]
    lists = [
        pltpu.make_async_copy(lab_hbm, lab_ref, load_sem.at[2]),
        pltpu.make_async_copy(val_hbm, val_ref, load_sem.at[3]),
    ]
    for copy in lists + loads:
        copy.start()

    barrier = pltpu.get_barrier_semaphore()

    @pl.loop(1, n)
    def _(d):
        pl.semaphore_signal(
            barrier, inc=1, device_id={"tm": lax.rem(me + d, n)}, device_id_type=pl.DeviceIdType.MESH
        )

    def remote(src, dst, send_sem, recv_sem, target):
        return pltpu.make_async_remote_copy(
            src_ref=src,
            dst_ref=dst,
            send_sem=send_sem,
            recv_sem=recv_sem,
            device_id={"tm": target},
            device_id_type=pl.DeviceIdType.MESH,
        )

    def drain(sem, ref):
        pltpu.make_async_copy(ref, ref, sem).wait()

    after = lax.rem(me + 1, n)

    for copy in lists:
        copy.wait()
    cycle = lax.broadcasted_iota(jnp.int32, (Q, 256), 0)
    members = jnp.zeros((Q, 256), jnp.float32)
    for g in range(groups):
        lab = lab_ref[:, pl.ds(g * 256, 256)]
        val = val_ref[:, pl.ds(g * 256, 256)].astype(jnp.float32)
        member = jnp.where(lab == cycle, val, 0.0)
        members = members + member
        wt[g] = jnp.concatenate([member.astype(jnp.bfloat16)] * 2, axis=0)

    acc = jnp.zeros((Q, 2 * frames), jnp.float32)
    for g in range(groups):
        if g % (groups // 2) == 0:
            loads[g * 2 // groups].wait()
        rhs = jnp.concatenate(split(x[:, pl.ds(g * 256, 256)]), axis=0)
        acc = acc + lax.dot_general(
            wt[g, pl.ds(0, Q)], rhs, (((1,), (1,)), ((), ())), preferred_element_type=jnp.float32
        )
    count = jnp.sum(members, axis=1, keepdims=True)
    inverse = (count / (acc[:, :frames] + acc[:, frames:])).T

    def normalise(first, count):
        lhs = jnp.concatenate(split(inverse[first : first + count]), axis=1)
        for g in range(groups):
            scale = jnp.dot(lhs, wt[g], preferred_element_type=jnp.float32)
            normed = x[pl.ds(first, count), pl.ds(g * 256, 256)] * scale
            series[0][2 * g, pl.ds(HALO + first, count), :] = normed[:, :LANES]
            series[0][2 * g + 1, pl.ds(HALO + first, count), :] = normed[:, LANES:]

    def halo(l, q):
        count = HALO if l == 0 else SUB
        part = pl.ds(q * (n // HALOS[l]), n // HALOS[l])
        return remote(
            series[l].at[part, pl.ds(frames >> l, count), :],
            series[l].at[part, pl.ds(0, count), :],
            sent.at[0],
            halo_recv.at[sum(HALOS[:l]) + q],
            after,
        )

    normalise(frames - HALO, HALO)
    pl.semaphore_wait(barrier, n - 1)

    @pl.when(me < n - 1)
    def _():
        for q in range(HALOS[0]):
            halo(0, q).start()

    normalise(0, frames - HALO)

    def coarse(c, carry):
        for l in range(1, LOCAL + 1):
            series[l][c, pl.ds(0 if l == LOCAL else HALO, frames >> l), :] = halve(
                series[l - 1], c, HALO, frames >> l
            )
        return carry

    each(0, n, coarse)

    @pl.when(me < n - 1)
    def _():
        for l in range(1, LOCAL):
            for q in range(HALOS[l]):
                halo(l, q).start()

    deep = frames >> LOCAL

    def spread():
        @pl.loop(1, n)
        def _(d):
            peer = lax.rem(me + d, n)
            remote(
                series[LOCAL].at[peer],
                far[0].at[0, pl.ds(pl.multiple_of(me * deep, SUB), deep), :],
                sent.at[2],
                got.at[0],
                peer,
            ).start()

    def inside(l):
        def one(c, carry):
            blocks = range(2, (frames >> l) // SUB)
            sums = add_lags(series[l], c, blocks, [None] * LAGS, HALO, -1)
            for k in range(LAGS):
                keepers[c, l * LAGS + k] = sums[k]
            return carry

        each(0, n, one)

    inside(0)
    inside(1)

    @pl.when(me == 0)
    def _():
        for l in range(LOCAL):
            count = HALO if l == 0 else SUB
            series[l][:, pl.ds(0, count), :] = jnp.zeros((n, count, LANES), jnp.float32)

    def parts(l, q):
        block = n // CHUNKS[l]
        return pl.ds(q * block, block)

    def sem(l, q):
        return sum(CHUNKS[:l]) + q

    def to_core(l, q):
        part = parts(l, q)
        return remote(
            partial.at[1 - side, l, part],
            inbox0.at[l, part],
            sent.at[3],
            core_recv.at[sem(l, q)],
            me + 1 - 2 * side,
        )

    def to_pair(l, q):
        part = parts(l, q)
        return remote(
            partial.at[side, l, part],
            inbox1.at[l // 2, part],
            sent.at[4 + l % 2],
            pair_recv.at[sem(l, q)],
            me + chip - 2 * chip * parity,
        )

    def half(y):
        return pl.ds(y * (n // 2), n // 2)

    def to_half():
        part = half(1 - parity)
        return remote(
            partial.at[side, 2, part],
            inbox1.at[1, part],
            sent.at[1],
            pair_recv.at[sem(2, 0)],
            me + chip - 2 * chip * parity,
        )

    def to_middle():
        part = half(parity)
        return remote(
            partial.at[side, 2, part], inbox.at[plane, part], sent.at[8], plane_recv.at[0], stack + side
        )

    def to_plane(l, q):
        part = parts(l, q)
        return remote(
            partial.at[side, l, part],
            inbox.at[plane, part],
            sent.at[6 + l],
            plane_recv.at[q],
            lax.rem(me, stack) + (l // 2) * stack,
        )

    def edges(l, q):
        block = n // CHUNKS[l]

        def edge(c, carry):
            if l > 0:
                series[l][c, pl.ds(SUB, SUB), :] = halve(series[l - 1], c, 0, SUB)
            sums = [keepers[c, l * LAGS + k] for k in range(LAGS)]
            sums = add_lags(series[l], c, range(2), sums, HALO, -1)
            for h in range(LAGS // SUB):
                partial[h, l, c] = fold_rows(sums[h * SUB : (h + 1) * SUB])
            return carry

        each(q * block, (q + 1) * block, edge)

    def compute(l):
        if l > 1:
            inside(l)

        for q in range(CHUNKS[l]):
            if q % (CHUNKS[l] // HALOS[l]) == 0:

                @pl.when(me > 0)
                def _():
                    halo(l, q * HALOS[l] // CHUNKS[l]).wait_recv()

            edges(l, q)
            to_core(l, q).start()

    def across(l):
        for q in range(CHUNKS[l]):
            part = parts(l, q)
            to_core(l, q).wait_recv()
            partial[side, l, part] = partial[side, l, part] + inbox0[l, part]

            @pl.when(parity != l % 2)
            def _():
                to_pair(l, q).start()

    def along(l):
        for q in range(CHUNKS[l]):

            @pl.when(parity == l % 2)
            def _():
                part = parts(l, q)
                to_pair(l, q).wait_recv()
                partial[side, l, part] = partial[side, l, part] + inbox1[l // 2, part]

                @pl.when(plane != l // 2)
                def _():
                    to_plane(l, q).start()

    compute(0)

    @pl.when(side == 0)
    def _():
        across(0)

    compute(1)
    spread()

    @pl.when(side > 0)
    def _():
        across(0)

    across(1)
    compute(2)
    to_core(2, 0).wait_recv()
    partial[side, 2] = partial[side, 2] + inbox0[2]
    to_half().start()
    def middle():
        to_half().wait_recv()
        partial[side, 2, half(parity)] = partial[side, 2, half(parity)] + inbox1[1, half(parity)]

        @pl.when((plane != 1) | (parity != 0))
        def _():
            to_middle().start()

    @pl.when(plane == 1)
    def _():
        middle()

    along(0)
    along(1)

    @pl.when(plane != 1)
    def _():
        middle()


    far[0][0, pl.ds(pl.multiple_of(me * deep, SUB), deep), :] = series[LOCAL][me]
    for i in range(LEVELS - LOCAL):
        count = total >> (LOCAL + i)
        far[i][0, pl.ds(count, 2 * SUB), :] = jnp.zeros((2 * SUB, LANES), jnp.float32)
    drain(got.at[0], far[0].at[0, pl.ds(0, (n - 1) * deep), :])
    lag = lax.broadcasted_iota(jnp.int32, (SUB, LANES), 0)

    def weight(l, h):
        return 1.0 / ((total >> l) - h * SUB - lag).astype(jnp.float32)

    for i in range(LEVELS - LOCAL):
        l = LOCAL + i
        count = total >> l
        if i > 0:
            far[i][0, pl.ds(0, count), :] = halve(far[i - 1], 0, 0, count)
        sums = add_lags(far[i], 0, range(count // SUB), [None] * LAGS)
        for h in range(LAGS // SUB):
            result[pl.ds(l * LAGS + h * SUB, SUB), :] = fold_rows(
                sums[h * SUB : (h + 1) * SUB]
            ) * weight(l, h)

    @pl.loop(1, n)
    def _(d):
        peer = lax.rem(me + d, n)

        @pl.when(peer >= keep)
        def _():
            remote(
                result.at[pl.ds(pl.multiple_of(peer * rows_out, SUB), rows_out), :],
                out_ref.at[:, pl.ds(pl.multiple_of(me * LANES, LANES), LANES)],
                sent.at[9],
                got.at[1],
                peer,
            ).start()


    @pl.when((plane == 1) & (parity == 0))
    def _():
        scale = 1.0 / ((total >> 2) - side * SUB - lag).astype(jnp.float32)
        drain(plane_recv.at[0], keepers.at[pl.ds(0, ((planes - 1) * n + n // 2) // SUB), pl.ds(0, SUB)])
        for c in range(n):
            rows = partial[side, 2, c] if c < n // 2 else inbox[1, c]
            for source in range(planes):
                if source != 1:
                    rows = rows + inbox[source, c]
            out_ref[:, pl.ds(c * LANES, LANES)] = rows * scale

    @pl.when((plane != 1) | (parity != 0))
    def _():
        drain(sent.at[8], inbox.at[0, pl.ds(0, n // 2)])

    for l in range(2):

        @pl.when((plane == l // 2) & (parity == l % 2))
        def _():
            scale = 1.0 / ((total >> l) - side * SUB - lag).astype(jnp.float32)
            for q in range(CHUNKS[l]):
                block = n // CHUNKS[l]
                drain(plane_recv.at[q], inbox.at[pl.ds(0, planes - 1), pl.ds(q * block, block)])
                for c in range(q * block, (q + 1) * block):
                    rows = partial[side, l, c]
                    for source in range(planes):
                        if source != l // 2:
                            rows = rows + inbox[source, c]
                    out_ref[:, pl.ds(c * LANES, LANES)] = rows * scale

        @pl.when((plane != l // 2) & (parity == l % 2))
        def _():
            drain(sent.at[6 + l], inbox.at[0])

    @pl.when(me >= keep)
    def _():
        out_ref[:, pl.ds(pl.multiple_of(me * LANES, LANES), LANES)] = result[
            pl.ds(pl.multiple_of(me * rows_out, SUB), rows_out), :
        ]
        drain(got.at[1], out_ref.at[:, pl.ds(0, (n - 1) * LANES)])
        drain(sent.at[9], out_ref.at[:, pl.ds(0, (n - keep - 1) * LANES)])

    @pl.when(me < keep)
    def _():
        drain(sent.at[9], out_ref.at[:, pl.ds(0, (n - keep) * LANES)])

    drain(sent.at[2], far[0].at[0, pl.ds(0, (n - 1) * deep), :])
    drain(sent.at[3], inbox0)
    drain(sent.at[1], inbox1.at[1, pl.ds(0, n // 2)])
    for p in range(2):

        @pl.when(parity != p)
        def _():
            drain(sent.at[4 + p], inbox1.at[0])

    @pl.when(me < n - 1)
    def _():
        drain(sent.at[0], series[0].at[:, pl.ds(0, SUB * (LOCAL + 1)), :])


def kernel_body(n, intensity, cycle_label, valid_mask):
    frames, pixels = intensity.shape
    f32 = jnp.float32
    dma = pltpu.SemaphoreType.DMA
    scratch = [
        pltpu.VMEM((frames, pixels), f32),
        pltpu.VMEM((pixels // 256, 2 * Q, 256), jnp.bfloat16),
        pltpu.VMEM((1, pixels), jnp.int32),
        pltpu.VMEM((1, pixels), jnp.int32),
    ]
    scratch += [pltpu.VMEM((n, (frames >> l) + 2 * SUB, LANES), f32) for l in range(LOCAL)]
    scratch += [pltpu.VMEM((n, frames >> LOCAL, LANES), f32)]
    scratch += [
        pltpu.VMEM((1, (n * frames >> l) + 2 * SUB, LANES), f32) for l in range(LOCAL, LEVELS)
    ]
    scratch += [
        pltpu.VMEM((n, LOCAL * LAGS, SUB, LANES), f32),
        pltpu.VMEM((2, LOCAL, n, SUB, LANES), f32),
        pltpu.VMEM((LOCAL, n, SUB, LANES), f32),
        pltpu.VMEM(((LOCAL + 1) // 2, n, SUB, LANES), f32),
        pltpu.VMEM((LEVELS // 2, n, SUB, LANES), f32),
        pltpu.VMEM((LEVELS * LAGS, LANES), f32),
        dma((4,)),
        dma((sum(HALOS),)),
        dma((sum(CHUNKS),)),
        dma((sum(CHUNKS),)),
        dma((max(CHUNKS),)),
        dma((10,)),
        dma((2,)),
    ]
    vmem = pl.BlockSpec(memory_space=pltpu.VMEM)
    return pl.pallas_call(
        functools.partial(kernel, n, frames),
        out_shape=pltpu.VMEM((LEVELS * LAGS // n, pixels), f32),
        in_specs=[pl.BlockSpec(memory_space=pl.ANY)] * 3,
        out_specs=vmem,
        scratch_shapes=scratch,
        compiler_params=pltpu.CompilerParams(collective_id=0, has_side_effects=True),
        name="multitau",
    )(intensity, cycle_label.reshape(1, pixels), valid_mask.reshape(1, pixels))


def route(intensity, cycle_label, valid_mask):
    n = lax.axis_size("tm")
    frames, pixels = intensity.shape
    fits = (
        lax.axis_size("pix") == 1
        and pixels == n * LANES
        and frames % (SUB << LOCAL) == 0
        and frames >> LOCAL >= 2 * SUB
        and LEVELS * LAGS == n * SUB
    )
    if fits:
        return kernel_body(n, intensity, cycle_label, valid_mask)
    return body(intensity, cycle_label, valid_mask)


def solution(mesh):
    placed = (P("tm", ("runs", "pix")), P(("runs", "pix")), P(("runs", "pix")))
    return jax.shard_map(
        route, mesh=mesh, in_specs=placed, out_specs=P("tm", ("runs", "pix")), check_vma=False
    )
```

```python
import functools
import jax
import jax.numpy as jnp
from jax import lax
from jax.experimental import pallas as pl
from jax.experimental.pallas import tpu as pltpu
from jax.sharding import PartitionSpec as P

Q = 128
LEVELS = 8
LAGS = 16


def coarsen(series):
    paired = series.reshape(series.shape[0] // 2, 2, series.shape[1])
    return (paired[:, 0] + paired[:, 1]) * 0.5


def level_rows(series, extension, total_frames):
    frames_here = series.shape[0]
    row_list = []
    for offset in range(extension.shape[0] + 1):
        inside = min(offset, frames_here)
        total = jnp.sum(series[: frames_here - inside] * series[inside:], axis=0)
        if offset > 0:
            tail_rows = series[frames_here - inside :]
            total = total + jnp.sum(tail_rows * extension[offset - inside : offset], axis=0)
        row_list.append(total / (total_frames - offset))
    return row_list


def pixel_rows(gathered):
    series = gathered[:, 0, :]
    row_list = []
    for height in range(LEVELS):
        if height > 0:
            series = coarsen(series)
        extension = jnp.zeros((LAGS - 1, series.shape[1]), jnp.float32)
        row_list = row_list + level_rows(series, extension, series.shape[0])
    return jnp.stack(row_list)


def body(intensity, cycle_label, valid_mask):
    valid_flag = valid_mask.astype(jnp.float32)
    member = (cycle_label[:, None] == jnp.arange(Q, dtype=jnp.int32)[None, :]).astype(jnp.float32)
    weighted = member * valid_flag[:, None]
    partial_sum = jnp.dot(intensity, weighted, precision=lax.Precision.HIGHEST)
    partial_count = jnp.sum(weighted, axis=0)
    cycle_sum, cycle_count = lax.psum((partial_sum, partial_count), "pix")
    cycle_mean = cycle_sum / cycle_count[None, :]
    per_pixel = lax.dot_general(
        cycle_mean, member, (((1,), (1,)), ((), ())), precision=lax.Precision.HIGHEST
    )
    normed = valid_flag[None, :] * intensity / per_pixel
    devices_tm = lax.axis_size("tm")
    tile_width = normed.shape[1] // devices_tm
    pieces = normed.reshape(normed.shape[0], devices_tm, tile_width)
    rows_local = pixel_rows(lax.all_to_all(pieces, "tm", split_axis=1, concat_axis=0, tiled=True))
    return lax.all_to_all(rows_local, "tm", split_axis=0, concat_axis=1, tiled=True)

LOCAL = 3
CHUNKS = (4, 4, 1)
HALOS = (4, 2, 1)
LANES = 128
SUB = 8
HALO = 2 * SUB
UNROLL = 4


def split(x):
    high = x.astype(jnp.bfloat16)
    return high, (x - high.astype(jnp.float32)).astype(jnp.bfloat16)


def fold_rows(parts):
    row = lax.broadcasted_iota(jnp.int32, (SUB, LANES), 0)
    for step in (4, 2, 1):
        keep = (row & step) == 0

        def swap(v, step=step, keep=keep):
            if step == 4:
                return pltpu.roll(v, 4, 0)
            return jnp.where(keep, pltpu.roll(v, SUB - step, 0), pltpu.roll(v, step, 0))

        parts = [
            jnp.where(keep, parts[i], parts[i + step]) + swap(jnp.where(keep, parts[i + step], parts[i]))
            for i in range(step)
        ]
    return parts[0]


def add_lags(ref, c, blocks, sums, first=0, sign=1):
    for b in blocks:
        base = ref[c, pl.ds(first + b * SUB, SUB), :]
        for k in range(LAGS):
            term = base * ref[c, pl.ds(first + b * SUB + sign * k, SUB), :]
            sums[k] = term if sums[k] is None else sums[k] + term
    return sums


def each(first, last, step):
    width = UNROLL
    while (last - first) % width:
        width //= 2

    def several(i, carry):
        for k in range(width):
            step(first + i * width + k, carry)
        return carry

    lax.fori_loop(0, (last - first) // width, several, 0)


def halve(ref, c, start, count):
    even = ref[c, pl.ds(start, count, stride=2), :]
    odd = ref[c, pl.ds(start + 1, count, stride=2), :]
    return (even + odd) * 0.5


def kernel(n, frames, x_hbm, lab_hbm, val_hbm, out_ref, *scratch):
    it = iter(scratch)
    x, wt, lab_ref, val_ref = (next(it) for _ in range(4))
    series = [next(it) for _ in range(LOCAL + 1)]
    far = [next(it) for _ in range(LEVELS - LOCAL)]
    keepers, partial, inbox0, inbox1, inbox, result = (next(it) for _ in range(6))
    load_sem, halo_recv, core_recv, pair_recv, plane_recv, sent, got = (next(it) for _ in range(7))
    me = lax.axis_index("tm")
    rows_out = LEVELS * LAGS // n
    total = n * frames
    groups = x.shape[1] // 256
    keep = LOCAL * LAGS // rows_out
    chip = LAGS // rows_out
    stack = 2 * chip
    planes = n // stack
    side, parity, plane = lax.rem(me, chip), lax.rem(me // chip, 2), me // stack

    half_width = x.shape[1] // 2
    loads = [
        pltpu.make_async_copy(
            x_hbm.at[:, pl.ds(g * half_width, half_width)],
            x.at[:, pl.ds(g * half_width, half_width)],
            load_sem.at[g],
        )
        for g in range(2)
    ]
    lists = [
        pltpu.make_async_copy(lab_hbm, lab_ref, load_sem.at[2]),
        pltpu.make_async_copy(val_hbm, val_ref, load_sem.at[3]),
    ]
    for copy in lists + loads:
        copy.start()

    barrier = pltpu.get_barrier_semaphore()

    @pl.loop(1, n)
    def _(d):
        pl.semaphore_signal(
            barrier, inc=1, device_id={"tm": lax.rem(me + d, n)}, device_id_type=pl.DeviceIdType.MESH
        )

    def remote(src, dst, send_sem, recv_sem, target):
        return pltpu.make_async_remote_copy(
            src_ref=src,
            dst_ref=dst,
            send_sem=send_sem,
            recv_sem=recv_sem,
            device_id={"tm": target},
            device_id_type=pl.DeviceIdType.MESH,
        )

    def drain(sem, ref):
        pltpu.make_async_copy(ref, ref, sem).wait()

    after = lax.rem(me + 1, n)

    for copy in lists:
        copy.wait()
    cycle = lax.broadcasted_iota(jnp.int32, (Q, 256), 0)
    members = jnp.zeros((Q, 256), jnp.float32)
    for g in range(groups):
        lab = lab_ref[:, pl.ds(g * 256, 256)]
        val = val_ref[:, pl.ds(g * 256, 256)].astype(jnp.float32)
        member = jnp.where(lab == cycle, val, 0.0)
        members = members + member
        wt[g] = jnp.concatenate([member.astype(jnp.bfloat16)] * 2, axis=0)

    acc = jnp.zeros((Q, 2 * frames), jnp.float32)
    for g in range(groups):
        if g % (groups // 2) == 0:
            loads[g * 2 // groups].wait()
        rhs = jnp.concatenate(split(x[:, pl.ds(g * 256, 256)]), axis=0)
        acc = acc + lax.dot_general(
            wt[g, pl.ds(0, Q)], rhs, (((1,), (1,)), ((), ())), preferred_element_type=jnp.float32
        )
    count = jnp.sum(members, axis=1, keepdims=True)
    inverse = (count / (acc[:, :frames] + acc[:, frames:])).T

    def normalise(first, count):
        lhs = jnp.concatenate(split(inverse[first : first + count]), axis=1)
        for g in range(groups):
            scale = jnp.dot(lhs, wt[g], preferred_element_type=jnp.float32)
            normed = x[pl.ds(first, count), pl.ds(g * 256, 256)] * scale
            series[0][2 * g, pl.ds(HALO + first, count), :] = normed[:, :LANES]
            series[0][2 * g + 1, pl.ds(HALO + first, count), :] = normed[:, LANES:]

    def halo(l, q):
        count = HALO if l == 0 else SUB
        part = pl.ds(q * (n // HALOS[l]), n // HALOS[l])
        return remote(
            series[l].at[part, pl.ds(frames >> l, count), :],
            series[l].at[part, pl.ds(0, count), :],
            sent.at[0],
            halo_recv.at[sum(HALOS[:l]) + q],
            after,
        )

    normalise(frames - HALO, HALO)
    pl.semaphore_wait(barrier, n - 1)

    @pl.when(me < n - 1)
    def _():
        for q in range(HALOS[0]):
            halo(0, q).start()

    normalise(0, frames - HALO)

    def coarse(c, carry):
        for l in range(1, LOCAL + 1):
            series[l][c, pl.ds(0 if l == LOCAL else HALO, frames >> l), :] = halve(
                series[l - 1], c, HALO, frames >> l
            )
        return carry

    each(0, n, coarse)

    @pl.when(me < n - 1)
    def _():
        for l in range(1, LOCAL):
            for q in range(HALOS[l]):
                halo(l, q).start()

    deep = frames >> LOCAL

    def spread():
        @pl.loop(1, n)
        def _(d):
            peer = lax.rem(me + d, n)
            remote(
                series[LOCAL].at[peer],
                far[0].at[0, pl.ds(pl.multiple_of(me * deep, SUB), deep), :],
                sent.at[2],
                got.at[0],
                peer,
            ).start()

    def inside(l):
        def one(c, carry):
            blocks = range(2, (frames >> l) // SUB)
            sums = add_lags(series[l], c, blocks, [None] * LAGS, HALO, -1)
            for k in range(LAGS):
                keepers[c, l * LAGS + k] = sums[k]
            return carry

        each(0, n, one)

    inside(0)
    inside(1)

    @pl.when(me == 0)
    def _():
        for l in range(LOCAL):
            count = HALO if l == 0 else SUB
            series[l][:, pl.ds(0, count), :] = jnp.zeros((n, count, LANES), jnp.float32)

    def parts(l, q):
        block = n // CHUNKS[l]
        return pl.ds(q * block, block)

    def sem(l, q):
        return sum(CHUNKS[:l]) + q

    def to_core(l, q):
        part = parts(l, q)
        return remote(
            partial.at[1 - side, l, part],
            inbox0.at[l, part],
            sent.at[3],
            core_recv.at[sem(l, q)],
            me + 1 - 2 * side,
        )

    def to_pair(l, q):
        part = parts(l, q)
        return remote(
            partial.at[side, l, part],
            inbox1.at[l // 2, part],
            sent.at[4 + l % 2],
            pair_recv.at[sem(l, q)],
            me + chip - 2 * chip * parity,
        )

    def half(y):
        return pl.ds(y * (n // 2), n // 2)

    def to_half():
        part = half(1 - parity)
        return remote(
            partial.at[side, 2, part],
            inbox1.at[1, part],
            sent.at[1],
            pair_recv.at[sem(2, 0)],
            me + chip - 2 * chip * parity,
        )

    def to_middle():
        part = half(parity)
        return remote(
            partial.at[side, 2, part], inbox.at[plane, part], sent.at[8], plane_recv.at[0], stack + side
        )

    def to_plane(l, q):
        part = parts(l, q)
        return remote(
            partial.at[side, l, part],
            inbox.at[plane, part],
            sent.at[6 + l],
            plane_recv.at[q],
            lax.rem(me, stack) + (l // 2) * stack,
        )

    def edges(l, q):
        block = n // CHUNKS[l]

        def edge(c, carry):
            if l > 0:
                series[l][c, pl.ds(SUB, SUB), :] = halve(series[l - 1], c, 0, SUB)
            sums = [keepers[c, l * LAGS + k] for k in range(LAGS)]
            sums = add_lags(series[l], c, range(2), sums, HALO, -1)
            for h in range(LAGS // SUB):
                partial[h, l, c] = fold_rows(sums[h * SUB : (h + 1) * SUB])
            return carry

        each(q * block, (q + 1) * block, edge)

    def compute(l):
        if l > 1:
            inside(l)

        for q in range(CHUNKS[l]):
            if q % (CHUNKS[l] // HALOS[l]) == 0:

                @pl.when(me > 0)
                def _():
                    halo(l, q * HALOS[l] // CHUNKS[l]).wait_recv()

            edges(l, q)
            to_core(l, q).start()

    def across(l):
        for q in range(CHUNKS[l]):
            part = parts(l, q)
            to_core(l, q).wait_recv()
            partial[side, l, part] = partial[side, l, part] + inbox0[l, part]

            @pl.when(parity != l % 2)
            def _():
                to_pair(l, q).start()

    def along(l):
        for q in range(CHUNKS[l]):

            @pl.when(parity == l % 2)
            def _():
                part = parts(l, q)
                to_pair(l, q).wait_recv()
                partial[side, l, part] = partial[side, l, part] + inbox1[l // 2, part]

                @pl.when(plane != l // 2)
                def _():
                    to_plane(l, q).start()

    compute(0)

    @pl.when(side == 0)
    def _():
        across(0)

    compute(1)
    spread()

    @pl.when(side > 0)
    def _():
        across(0)

    across(1)
    compute(2)
    to_core(2, 0).wait_recv()
    partial[side, 2] = partial[side, 2] + inbox0[2]
    to_half().start()
    def middle():
        to_half().wait_recv()
        partial[side, 2, half(parity)] = partial[side, 2, half(parity)] + inbox1[1, half(parity)]

        @pl.when((plane != 1) | (parity != 0))
        def _():
            to_middle().start()

    @pl.when(plane == 1)
    def _():
        middle()

    along(0)
    along(1)

    @pl.when(plane != 1)
    def _():
        middle()


    far[0][0, pl.ds(pl.multiple_of(me * deep, SUB), deep), :] = series[LOCAL][me]
    for i in range(LEVELS - LOCAL):
        count = total >> (LOCAL + i)
        far[i][0, pl.ds(count, 2 * SUB), :] = jnp.zeros((2 * SUB, LANES), jnp.float32)
    drain(got.at[0], far[0].at[0, pl.ds(0, (n - 1) * deep), :])
    lag = lax.broadcasted_iota(jnp.int32, (SUB, LANES), 0)

    def weight(l, h):
        return 1.0 / ((total >> l) - h * SUB - lag).astype(jnp.float32)

    for i in range(LEVELS - LOCAL):
        l = LOCAL + i
        count = total >> l
        if i > 0:
            far[i][0, pl.ds(0, count), :] = halve(far[i - 1], 0, 0, count)
        sums = add_lags(far[i], 0, range(count // SUB), [None] * LAGS)
        for h in range(LAGS // SUB):
            result[pl.ds(l * LAGS + h * SUB, SUB), :] = fold_rows(
                sums[h * SUB : (h + 1) * SUB]
            ) * weight(l, h)

    @pl.loop(1, n)
    def _(d):
        peer = lax.rem(me + d, n)

        @pl.when(peer >= keep)
        def _():
            remote(
                result.at[pl.ds(pl.multiple_of(peer * rows_out, SUB), rows_out), :],
                out_ref.at[:, pl.ds(pl.multiple_of(me * LANES, LANES), LANES)],
                sent.at[9],
                got.at[1],
                peer,
            ).start()


    @pl.when((plane == 1) & (parity == 0))
    def _():
        scale = 1.0 / ((total >> 2) - side * SUB - lag).astype(jnp.float32)
        drain(plane_recv.at[0], keepers.at[pl.ds(0, ((planes - 1) * n + n // 2) // SUB), pl.ds(0, SUB)])
        for c in range(n):
            rows = partial[side, 2, c] if c < n // 2 else inbox[1, c]
            for source in range(planes):
                if source != 1:
                    rows = rows + inbox[source, c]
            out_ref[:, pl.ds(c * LANES, LANES)] = rows * scale

    @pl.when((plane != 1) | (parity != 0))
    def _():
        drain(sent.at[8], inbox.at[0, pl.ds(0, n // 2)])

    for l in range(2):

        @pl.when((plane == l // 2) & (parity == l % 2))
        def _():
            scale = 1.0 / ((total >> l) - side * SUB - lag).astype(jnp.float32)
            for q in range(CHUNKS[l]):
                block = n // CHUNKS[l]
                drain(plane_recv.at[q], inbox.at[pl.ds(0, planes - 1), pl.ds(q * block, block)])
                for c in range(q * block, (q + 1) * block):
                    rows = partial[side, l, c]
                    for source in range(planes):
                        if source != l // 2:
                            rows = rows + inbox[source, c]
                    out_ref[:, pl.ds(c * LANES, LANES)] = rows * scale

        @pl.when((plane != l // 2) & (parity == l % 2))
        def _():
            drain(sent.at[6 + l], inbox.at[0])

    @pl.when(me >= keep)
    def _():
        out_ref[:, pl.ds(pl.multiple_of(me * LANES, LANES), LANES)] = result[
            pl.ds(pl.multiple_of(me * rows_out, SUB), rows_out), :
        ]
        drain(got.at[1], out_ref.at[:, pl.ds(0, (n - 1) * LANES)])
        drain(sent.at[9], out_ref.at[:, pl.ds(0, (n - keep - 1) * LANES)])

    @pl.when(me < keep)
    def _():
        drain(sent.at[9], out_ref.at[:, pl.ds(0, (n - keep) * LANES)])

    drain(sent.at[2], far[0].at[0, pl.ds(0, (n - 1) * deep), :])
    drain(sent.at[3], inbox0)
    drain(sent.at[1], inbox1.at[1, pl.ds(0, n // 2)])
    for p in range(2):

        @pl.when(parity != p)
        def _():
            drain(sent.at[4 + p], inbox1.at[0])

    @pl.when(me < n - 1)
    def _():
        drain(sent.at[0], series[0].at[:, pl.ds(0, SUB * (LOCAL + 1)), :])


def kernel_body(n, intensity, cycle_label, valid_mask):
    frames, pixels = intensity.shape
    f32 = jnp.float32
    dma = pltpu.SemaphoreType.DMA
    scratch = [
        pltpu.VMEM((frames, pixels), f32),
        pltpu.VMEM((pixels // 256, 2 * Q, 256), jnp.bfloat16),
        pltpu.VMEM((1, pixels), jnp.int32),
        pltpu.VMEM((1, pixels), jnp.int32),
    ]
    scratch += [pltpu.VMEM((n, (frames >> l) + 3 * SUB, LANES), f32) for l in range(LOCAL)]
    scratch += [pltpu.VMEM((n, frames >> LOCAL, LANES), f32)]
    scratch += [
        pltpu.VMEM((1, (n * frames >> l) + 2 * SUB, LANES), f32) for l in range(LOCAL, LEVELS)
    ]
    scratch += [
        pltpu.VMEM((n, LOCAL * LAGS, SUB, LANES), f32),
        pltpu.VMEM((2, LOCAL, n, SUB, LANES), f32),
        pltpu.VMEM((LOCAL, n, SUB, LANES), f32),
        pltpu.VMEM(((LOCAL + 1) // 2, n, SUB, LANES), f32),
        pltpu.VMEM((LEVELS // 2, n, SUB, LANES), f32),
        pltpu.VMEM((LEVELS * LAGS, LANES), f32),
        dma((4,)),
        dma((sum(HALOS),)),
        dma((sum(CHUNKS),)),
        dma((sum(CHUNKS),)),
        dma((max(CHUNKS),)),
        dma((10,)),
        dma((2,)),
    ]
    vmem = pl.BlockSpec(memory_space=pltpu.VMEM)
    return pl.pallas_call(
        functools.partial(kernel, n, frames),
        out_shape=pltpu.VMEM((LEVELS * LAGS // n, pixels), f32),
        in_specs=[pl.BlockSpec(memory_space=pl.ANY)] * 3,
        out_specs=vmem,
        scratch_shapes=scratch,
        compiler_params=pltpu.CompilerParams(collective_id=0, has_side_effects=True),
        name="multitau",
    )(intensity, cycle_label.reshape(1, pixels), valid_mask.reshape(1, pixels))


def route(intensity, cycle_label, valid_mask):
    n = lax.axis_size("tm")
    frames, pixels = intensity.shape
    fits = (
        lax.axis_size("pix") == 1
        and pixels == n * LANES
        and frames % (SUB << LOCAL) == 0
        and frames >> LOCAL >= 2 * SUB
        and LEVELS * LAGS == n * SUB
    )
    if fits:
        return kernel_body(n, intensity, cycle_label, valid_mask)
    return body(intensity, cycle_label, valid_mask)


def solution(mesh):
    placed = (P("tm", ("runs", "pix")), P(("runs", "pix")), P(("runs", "pix")))
    return jax.shard_map(
        route, mesh=mesh, in_specs=placed, out_specs=P("tm", ("runs", "pix")), check_vma=False
    )
```

```python
import functools
import jax
import jax.numpy as jnp
from jax import lax
from jax.experimental import pallas as pl
from jax.experimental.pallas import tpu as pltpu
from jax.sharding import PartitionSpec as P

Q = 128
LEVELS = 8
LAGS = 16


def coarsen(series):
    paired = series.reshape(series.shape[0] // 2, 2, series.shape[1])
    return (paired[:, 0] + paired[:, 1]) * 0.5


def level_rows(series, extension, total_frames):
    frames_here = series.shape[0]
    row_list = []
    for offset in range(extension.shape[0] + 1):
        inside = min(offset, frames_here)
        total = jnp.sum(series[: frames_here - inside] * series[inside:], axis=0)
        if offset > 0:
            tail_rows = series[frames_here - inside :]
            total = total + jnp.sum(tail_rows * extension[offset - inside : offset], axis=0)
        row_list.append(total / (total_frames - offset))
    return row_list


def pixel_rows(gathered):
    series = gathered[:, 0, :]
    row_list = []
    for height in range(LEVELS):
        if height > 0:
            series = coarsen(series)
        extension = jnp.zeros((LAGS - 1, series.shape[1]), jnp.float32)
        row_list = row_list + level_rows(series, extension, series.shape[0])
    return jnp.stack(row_list)


def body(intensity, cycle_label, valid_mask):
    valid_flag = valid_mask.astype(jnp.float32)
    member = (cycle_label[:, None] == jnp.arange(Q, dtype=jnp.int32)[None, :]).astype(jnp.float32)
    weighted = member * valid_flag[:, None]
    partial_sum = jnp.dot(intensity, weighted, precision=lax.Precision.HIGHEST)
    partial_count = jnp.sum(weighted, axis=0)
    cycle_sum, cycle_count = lax.psum((partial_sum, partial_count), "pix")
    cycle_mean = cycle_sum / cycle_count[None, :]
    per_pixel = lax.dot_general(
        cycle_mean, member, (((1,), (1,)), ((), ())), precision=lax.Precision.HIGHEST
    )
    normed = valid_flag[None, :] * intensity / per_pixel
    devices_tm = lax.axis_size("tm")
    tile_width = normed.shape[1] // devices_tm
    pieces = normed.reshape(normed.shape[0], devices_tm, tile_width)
    rows_local = pixel_rows(lax.all_to_all(pieces, "tm", split_axis=1, concat_axis=0, tiled=True))
    return lax.all_to_all(rows_local, "tm", split_axis=0, concat_axis=1, tiled=True)

LOCAL = 3
CHUNKS = (4, 4, 1)
HALOS = (4, 2, 1)
LANES = 128
SUB = 8
HALO = 2 * SUB
UNROLL = 4


def split(x):
    high = x.astype(jnp.bfloat16)
    return high, (x - high.astype(jnp.float32)).astype(jnp.bfloat16)


def fold_rows(parts):
    row = lax.broadcasted_iota(jnp.int32, (SUB, LANES), 0)
    for step in (4, 2, 1):
        keep = (row & step) == 0

        def swap(v, step=step, keep=keep):
            if step == 4:
                return pltpu.roll(v, 4, 0)
            return jnp.where(keep, pltpu.roll(v, SUB - step, 0), pltpu.roll(v, step, 0))

        parts = [
            jnp.where(keep, parts[i], parts[i + step]) + swap(jnp.where(keep, parts[i + step], parts[i]))
            for i in range(step)
        ]
    return parts[0]


def add_lags(ref, c, blocks, sums, first=0, sign=1):
    for b in blocks:
        base = ref[c, pl.ds(first + b * SUB, SUB), :]
        for k in range(LAGS):
            term = base * ref[c, pl.ds(first + b * SUB + sign * k, SUB), :]
            sums[k] = term if sums[k] is None else sums[k] + term
    return sums


def each(first, last, step):
    width = UNROLL
    while (last - first) % width:
        width //= 2

    def several(i, carry):
        for k in range(width):
            step(first + i * width + k, carry)
        return carry

    lax.fori_loop(0, (last - first) // width, several, 0)


def halve(ref, c, start, count):
    even = ref[c, pl.ds(start, count, stride=2), :]
    odd = ref[c, pl.ds(start + 1, count, stride=2), :]
    return (even + odd) * 0.5


def kernel(n, frames, x_hbm, lab_hbm, val_hbm, out_ref, *scratch):
    it = iter(scratch)
    x, wt, lab_ref, val_ref = (next(it) for _ in range(4))
    series = [next(it) for _ in range(LOCAL + 1)]
    far = [next(it) for _ in range(LEVELS - LOCAL)]
    keepers, partial, inbox0, inbox1, inbox, result = (next(it) for _ in range(6))
    load_sem, halo_recv, core_recv, pair_recv, plane_recv, sent, got = (next(it) for _ in range(7))
    me = lax.axis_index("tm")
    rows_out = LEVELS * LAGS // n
    total = n * frames
    groups = x.shape[1] // 256
    keep = LOCAL * LAGS // rows_out
    chip = LAGS // rows_out
    stack = 2 * chip
    planes = n // stack
    side, parity, plane = lax.rem(me, chip), lax.rem(me // chip, 2), me // stack

    half_width = x.shape[1] // 2
    loads = [
        pltpu.make_async_copy(
            x_hbm.at[:, pl.ds(g * half_width, half_width)],
            x.at[:, pl.ds(g * half_width, half_width)],
            load_sem.at[g],
        )
        for g in range(2)
    ]
    lists = [
        pltpu.make_async_copy(lab_hbm, lab_ref, load_sem.at[2]),
        pltpu.make_async_copy(val_hbm, val_ref, load_sem.at[3]),
    ]
    for copy in lists + loads:
        copy.start()

    barrier = pltpu.get_barrier_semaphore()

    @pl.loop(1, n)
    def _(d):
        pl.semaphore_signal(
            barrier, inc=1, device_id={"tm": lax.rem(me + d, n)}, device_id_type=pl.DeviceIdType.MESH
        )

    def remote(src, dst, send_sem, recv_sem, target):
        return pltpu.make_async_remote_copy(
            src_ref=src,
            dst_ref=dst,
            send_sem=send_sem,
            recv_sem=recv_sem,
            device_id={"tm": target},
            device_id_type=pl.DeviceIdType.MESH,
        )

    def drain(sem, ref):
        pltpu.make_async_copy(ref, ref, sem).wait()

    after = lax.rem(me + 1, n)

    for copy in lists:
        copy.wait()
    cycle = lax.broadcasted_iota(jnp.int32, (Q, 256), 0)
    members = jnp.zeros((Q, 256), jnp.float32)
    for g in range(groups):
        lab = lab_ref[:, pl.ds(g * 256, 256)]
        val = val_ref[:, pl.ds(g * 256, 256)].astype(jnp.float32)
        member = jnp.where(lab == cycle, val, 0.0)
        members = members + member
        wt[g] = jnp.concatenate([member.astype(jnp.bfloat16)] * 2, axis=0)

    acc = jnp.zeros((Q, 2 * frames), jnp.float32)
    for g in range(groups):
        if g % (groups // 2) == 0:
            loads[g * 2 // groups].wait()
        rhs = jnp.concatenate(split(x[:, pl.ds(g * 256, 256)]), axis=0)
        acc = acc + lax.dot_general(
            wt[g, pl.ds(0, Q)], rhs, (((1,), (1,)), ((), ())), preferred_element_type=jnp.float32
        )
    count = jnp.sum(members, axis=1, keepdims=True)
    inverse = (count / (acc[:, :frames] + acc[:, frames:])).T

    def normalise(first, count):
        lhs = jnp.concatenate(split(inverse[first : first + count]), axis=1)
        for g in range(groups):
            scale = jnp.dot(lhs, wt[g], preferred_element_type=jnp.float32)
            normed = x[pl.ds(first, count), pl.ds(g * 256, 256)] * scale
            series[0][2 * g, pl.ds(HALO + first, count), :] = normed[:, :LANES]
            series[0][2 * g + 1, pl.ds(HALO + first, count), :] = normed[:, LANES:]

    def halo(l, q):
        count = HALO if l == 0 else SUB
        part = pl.ds(q * (n // HALOS[l]), n // HALOS[l])
        return remote(
            series[l].at[part, pl.ds(frames >> l, count), :],
            series[l].at[part, pl.ds(0, count), :],
            sent.at[0],
            halo_recv.at[sum(HALOS[:l]) + q],
            after,
        )

    normalise(frames - HALO, HALO)
    pl.semaphore_wait(barrier, n - 1)

    @pl.when(me < n - 1)
    def _():
        for q in range(HALOS[0]):
            halo(0, q).start()

    normalise(0, frames - HALO)

    def coarse(c, carry):
        for l in range(1, LOCAL + 1):
            series[l][c, pl.ds(0 if l == LOCAL else HALO, frames >> l), :] = halve(
                series[l - 1], c, HALO, frames >> l
            )
        return carry

    each(0, n, coarse)

    @pl.when(me < n - 1)
    def _():
        for l in range(1, LOCAL):
            for q in range(HALOS[l]):
                halo(l, q).start()

    deep = frames >> LOCAL

    def spread():
        @pl.loop(1, n)
        def _(d):
            peer = lax.rem(me + d, n)
            remote(
                series[LOCAL].at[peer],
                far[0].at[0, pl.ds(pl.multiple_of(me * deep, SUB), deep), :],
                sent.at[2],
                got.at[0],
                peer,
            ).start()

    def inside(l):
        def one(c, carry):
            blocks = range(2, (frames >> l) // SUB)
            sums = add_lags(series[l], c, blocks, [None] * LAGS, HALO, -1)
            for k in range(LAGS):
                keepers[c, l * LAGS + k] = sums[k]
            return carry

        each(0, n, one)

    inside(0)
    inside(1)

    @pl.when(me == 0)
    def _():
        for l in range(LOCAL):
            count = HALO if l == 0 else SUB
            series[l][:, pl.ds(0, count), :] = jnp.zeros((n, count, LANES), jnp.float32)

    def parts(l, q):
        block = n // CHUNKS[l]
        return pl.ds(q * block, block)

    def sem(l, q):
        return sum(CHUNKS[:l]) + q

    def to_core(l, q):
        part = parts(l, q)
        return remote(
            partial.at[1 - side, l, part],
            inbox0.at[l, part],
            sent.at[3],
            core_recv.at[sem(l, q)],
            me + 1 - 2 * side,
        )

    def to_pair(l, q):
        part = parts(l, q)
        return remote(
            partial.at[side, l, part],
            inbox1.at[l // 2, part],
            sent.at[4],
            pair_recv.at[sem(l, q)],
            me + chip - 2 * chip * parity,
        )

    def half(y):
        return pl.ds(y * (n // 2), n // 2)

    def to_half():
        part = half(1 - parity)
        return remote(
            partial.at[side, 2, part],
            inbox1.at[1, part],
            sent.at[1],
            pair_recv.at[sem(2, 0)],
            me + chip - 2 * chip * parity,
        )

    def to_middle():
        part = half(parity)
        return remote(
            partial.at[side, 2, part], inbox.at[plane, part], sent.at[6], plane_recv.at[0], stack + side
        )

    def to_plane(l, q):
        part = parts(l, q)
        return remote(
            partial.at[side, l, part],
            inbox.at[plane, part],
            sent.at[5],
            plane_recv.at[q],
            lax.rem(me, stack) + (l // 2) * stack,
        )

    def edges(l, q):
        block = n // CHUNKS[l]

        def edge(c, carry):
            if l > 0:
                series[l][c, pl.ds(SUB, SUB), :] = halve(series[l - 1], c, 0, SUB)
            sums = [keepers[c, l * LAGS + k] for k in range(LAGS)]
            sums = add_lags(series[l], c, range(2), sums, HALO, -1)
            for h in range(LAGS // SUB):
                partial[h, l, c] = fold_rows(sums[h * SUB : (h + 1) * SUB])
            return carry

        each(q * block, (q + 1) * block, edge)

    def compute(l):
        if l > 1:
            inside(l)

        for q in range(CHUNKS[l]):
            if q % (CHUNKS[l] // HALOS[l]) == 0:

                @pl.when(me > 0)
                def _():
                    halo(l, q * HALOS[l] // CHUNKS[l]).wait_recv()

            edges(l, q)
            to_core(l, q).start()

    def across(l):
        for q in range(CHUNKS[l]):
            part = parts(l, q)
            to_core(l, q).wait_recv()
            partial[side, l, part] = partial[side, l, part] + inbox0[l, part]

            @pl.when(parity != l % 2)
            def _():
                to_pair(l, q).start()

    def along(l):
        for q in range(CHUNKS[l]):

            @pl.when(parity == l % 2)
            def _():
                part = parts(l, q)
                to_pair(l, q).wait_recv()
                partial[side, l, part] = partial[side, l, part] + inbox1[l // 2, part]

                @pl.when(plane != l // 2)
                def _():
                    to_plane(l, q).start()

    compute(0)

    @pl.when(side == 0)
    def _():
        across(0)

    compute(1)
    spread()

    @pl.when(side > 0)
    def _():
        across(0)

    across(1)
    compute(2)
    to_core(2, 0).wait_recv()
    partial[side, 2] = partial[side, 2] + inbox0[2]
    to_half().start()
    def middle():
        to_half().wait_recv()
        partial[side, 2, half(parity)] = partial[side, 2, half(parity)] + inbox1[1, half(parity)]

        @pl.when((plane != 1) | (parity != 0))
        def _():
            to_middle().start()

    @pl.when(plane == 1)
    def _():
        middle()

    along(0)
    along(1)

    @pl.when(plane != 1)
    def _():
        middle()


    far[0][0, pl.ds(pl.multiple_of(me * deep, SUB), deep), :] = series[LOCAL][me]
    for i in range(LEVELS - LOCAL):
        count = total >> (LOCAL + i)
        far[i][0, pl.ds(count, 2 * SUB), :] = jnp.zeros((2 * SUB, LANES), jnp.float32)
    drain(got.at[0], far[0].at[0, pl.ds(0, (n - 1) * deep), :])
    lag = lax.broadcasted_iota(jnp.int32, (SUB, LANES), 0)

    def weight(l, h):
        return 1.0 / ((total >> l) - h * SUB - lag).astype(jnp.float32)

    for i in range(LEVELS - LOCAL):
        l = LOCAL + i
        count = total >> l
        if i > 0:
            far[i][0, pl.ds(0, count), :] = halve(far[i - 1], 0, 0, count)
        sums = add_lags(far[i], 0, range(count // SUB), [None] * LAGS)
        for h in range(LAGS // SUB):
            result[pl.ds(l * LAGS + h * SUB, SUB), :] = fold_rows(
                sums[h * SUB : (h + 1) * SUB]
            ) * weight(l, h)

    @pl.loop(1, n)
    def _(d):
        peer = lax.rem(me + d, n)

        @pl.when(peer >= keep)
        def _():
            remote(
                result.at[pl.ds(pl.multiple_of(peer * rows_out, SUB), rows_out), :],
                out_ref.at[:, pl.ds(pl.multiple_of(me * LANES, LANES), LANES)],
                sent.at[7],
                got.at[1],
                peer,
            ).start()


    @pl.when((plane == 1) & (parity == 0))
    def _():
        scale = 1.0 / ((total >> 2) - side * SUB - lag).astype(jnp.float32)
        drain(plane_recv.at[0], keepers.at[pl.ds(0, ((planes - 1) * n + n // 2) // SUB), pl.ds(0, SUB)])
        for c in range(n):
            rows = partial[side, 2, c] if c < n // 2 else inbox[1, c]
            for source in range(planes):
                if source != 1:
                    rows = rows + inbox[source, c]
            out_ref[:, pl.ds(c * LANES, LANES)] = rows * scale

    @pl.when((plane != 1) | (parity != 0))
    def _():
        drain(sent.at[6], inbox.at[0, pl.ds(0, n // 2)])

    for l in range(2):

        @pl.when((plane == l // 2) & (parity == l % 2))
        def _():
            scale = 1.0 / ((total >> l) - side * SUB - lag).astype(jnp.float32)
            for q in range(CHUNKS[l]):
                block = n // CHUNKS[l]
                drain(plane_recv.at[q], inbox.at[pl.ds(0, planes - 1), pl.ds(q * block, block)])
                for c in range(q * block, (q + 1) * block):
                    rows = partial[side, l, c]
                    for source in range(planes):
                        if source != l // 2:
                            rows = rows + inbox[source, c]
                    out_ref[:, pl.ds(c * LANES, LANES)] = rows * scale

        @pl.when((plane != l // 2) & (parity == l % 2))
        def _():
            drain(sent.at[5], inbox.at[0])

    @pl.when(me >= keep)
    def _():
        out_ref[:, pl.ds(pl.multiple_of(me * LANES, LANES), LANES)] = result[
            pl.ds(pl.multiple_of(me * rows_out, SUB), rows_out), :
        ]
        drain(got.at[1], out_ref.at[:, pl.ds(0, (n - 1) * LANES)])
        drain(sent.at[7], out_ref.at[:, pl.ds(0, (n - keep - 1) * LANES)])

    @pl.when(me < keep)
    def _():
        drain(sent.at[7], out_ref.at[:, pl.ds(0, (n - keep) * LANES)])

    drain(sent.at[2], far[0].at[0, pl.ds(0, (n - 1) * deep), :])
    drain(sent.at[3], inbox0)
    drain(sent.at[1], inbox1.at[1, pl.ds(0, n // 2)])
    for p in range(2):

        @pl.when(parity != p)
        def _():
            drain(sent.at[4], inbox1.at[0])

    @pl.when(me < n - 1)
    def _():
        drain(sent.at[0], series[0].at[:, pl.ds(0, SUB * (LOCAL + 1)), :])


def kernel_body(n, intensity, cycle_label, valid_mask):
    frames, pixels = intensity.shape
    f32 = jnp.float32
    dma = pltpu.SemaphoreType.DMA
    scratch = [
        pltpu.VMEM((frames, pixels), f32),
        pltpu.VMEM((pixels // 256, 2 * Q, 256), jnp.bfloat16),
        pltpu.VMEM((1, pixels), jnp.int32),
        pltpu.VMEM((1, pixels), jnp.int32),
    ]
    scratch += [pltpu.VMEM((n, (frames >> l) + 3 * SUB, LANES), f32) for l in range(LOCAL)]
    scratch += [pltpu.VMEM((n, frames >> LOCAL, LANES), f32)]
    scratch += [
        pltpu.VMEM((1, (n * frames >> l) + 2 * SUB, LANES), f32) for l in range(LOCAL, LEVELS)
    ]
    scratch += [
        pltpu.VMEM((n, LOCAL * LAGS, SUB, LANES), f32),
        pltpu.VMEM((2, LOCAL, n, SUB, LANES), f32),
        pltpu.VMEM((LOCAL, n, SUB, LANES), f32),
        pltpu.VMEM(((LOCAL + 1) // 2, n, SUB, LANES), f32),
        pltpu.VMEM((LEVELS // 2, n, SUB, LANES), f32),
        pltpu.VMEM((LEVELS * LAGS, LANES), f32),
        dma((4,)),
        dma((sum(HALOS),)),
        dma((sum(CHUNKS),)),
        dma((sum(CHUNKS),)),
        dma((max(CHUNKS),)),
        dma((8,)),
        dma((2,)),
    ]
    vmem = pl.BlockSpec(memory_space=pltpu.VMEM)
    return pl.pallas_call(
        functools.partial(kernel, n, frames),
        out_shape=pltpu.VMEM((LEVELS * LAGS // n, pixels), f32),
        in_specs=[pl.BlockSpec(memory_space=pl.ANY)] * 3,
        out_specs=vmem,
        scratch_shapes=scratch,
        compiler_params=pltpu.CompilerParams(collective_id=0, has_side_effects=True),
        name="multitau",
    )(intensity, cycle_label.reshape(1, pixels), valid_mask.reshape(1, pixels))


def route(intensity, cycle_label, valid_mask):
    n = lax.axis_size("tm")
    frames, pixels = intensity.shape
    fits = (
        lax.axis_size("pix") == 1
        and pixels == n * LANES
        and frames % (SUB << LOCAL) == 0
        and frames >> LOCAL >= 2 * SUB
        and LEVELS * LAGS == n * SUB
    )
    if fits:
        return kernel_body(n, intensity, cycle_label, valid_mask)
    return body(intensity, cycle_label, valid_mask)


def solution(mesh):
    placed = (P("tm", ("runs", "pix")), P(("runs", "pix")), P(("runs", "pix")))
    return jax.shard_map(
        route, mesh=mesh, in_specs=placed, out_specs=P("tm", ("runs", "pix")), check_vma=False
    )
```
